32 devices in a mesh: ax: 16 (over z, x, core), az: 2 (over y).
Axes of the slice: x: 2, y: 2, z: 4, core: 2. Of those that a mesh axis runs over, the one named last changes fastest.
Arguments:
- conserved: float32 [64, 5, 32, 512], P('ax', None, None, 'az'), may hold values from -1.1 to 6.2, as said below
- cycle_modes: int32 [32], replicated, may hold values from 1 to 64, as said below
- filtered_cycles: int32 [64], P('ax'), may hold values from 1 to 32, as said below
Outputs:
- stepped: float32 [64, 5, 32, 512], P('ax', None, None, 'az')
The draws below stay inside these ranges and needn't reach their ends.
Inputs may be any that keep to these rules, and one draw needn't show every extreme that they name: `conserved`: density is at least 0.3 and pressure at least 0.02 in every cell. `cycle_modes`: 64 and 1 both occur. `filtered_cycles`: 32 and 1 both occur.
All inputs are finite; a program needn't handle non-finite values.
Results may differ from the reference program's by a relative error of at most 0.0003.
Values sent between devices are 32-bit elements; how exact they have to be, the bound alone decides.
No kernel may reach another device: no remote copies, remote signals or barrier semaphores. Data moves between devices by JAX's collectives and lax.ppermute only.
A program may use at most 64 MiB of HBM per device.

```python
import math
import jax
import jax.numpy as jnp
from jax import lax

NR = 32
NT = 512
NRF = 32
MODE_MOST = 64
NX = 64


def draw_conserved(key, part):
    keys = jax.random.split(key, 5)
    grid_shape = (NX, NR, NT)
    density = jnp.exp(jax.random.uniform(keys[0], grid_shape, jnp.float32, math.log(0.5), math.log(2.0)))
    pressure = jnp.exp(jax.random.uniform(keys[4], grid_shape, jnp.float32, math.log(0.03), math.log(0.1)))
    axial_vel = 1.5 + 0.2 * jnp.clip(jax.random.normal(keys[1], grid_shape, jnp.float32), -2.5, 2.5)
    radial_vel = 0.14 * jnp.clip(jax.random.normal(keys[2], grid_shape, jnp.float32), -2.5, 2.5)
    swirl_vel = 0.14 * jnp.clip(jax.random.normal(keys[3], grid_shape, jnp.float32), -2.5, 2.5)
    energy = pressure / 0.4 + 0.5 * density * (axial_vel * axial_vel + radial_vel * radial_vel + swirl_vel * swirl_vel)
    fields = jnp.stack([density, density * axial_vel, density * radial_vel, density * swirl_vel, energy], axis=1)
    return fields.astype(jnp.float32)


def draw_cycle_modes(key, part):
    keys = jax.random.split(jax.random.fold_in(key, 11), 3)
    base_modes = jax.random.randint(keys[0], (NRF,), 1, MODE_MOST + 1)
    top_cycle = jax.random.randint(keys[1], (), 0, NRF)
    low_cycle = (top_cycle + 1 + jax.random.randint(keys[2], (), 0, NRF - 1)) % NRF
    cycle_ids = jnp.arange(NRF, dtype=jnp.int32)
    modes = jnp.where(cycle_ids == top_cycle, MODE_MOST, jnp.where(cycle_ids == low_cycle, 1, base_modes))
    return modes.astype(jnp.int32)


def draw_filtered_cycles(key, part):
    keys = jax.random.split(jax.random.fold_in(key, 23), 3)
    base_counts = jax.random.randint(keys[0], (NX,), 1, NRF + 1)
    top_station = jax.random.randint(keys[1], (), 0, NX)
    low_station = (top_station + 1 + jax.random.randint(keys[2], (), 0, NX - 1)) % NX
    station_ids = jnp.arange(NX, dtype=jnp.int32)
    counts = jnp.where(station_ids == top_station, NRF, jnp.where(station_ids == low_station, 1, base_counts))
    return counts.astype(jnp.int32)


def setup_inputs(seed: int = 0) -> dict:
    arg_keys = jax.random.split(jax.random.key(seed), 4)
    return {
        "conserved": draw_conserved(jax.random.fold_in(arg_keys[3], 71), 0),
        "cycle_modes": draw_cycle_modes(jax.random.fold_in(arg_keys[3], 71), 0),
        "filtered_cycles": draw_filtered_cycles(jax.random.fold_in(arg_keys[3], 71), 0),
    }


STENCIL = (0.8, -0.2, 4.0 / 105.0, -1.0 / 280.0)
GAS_FACTOR = 0.4
TIME_STEP = 0.1


def velocities(fields):
    density = fields[:, 0]
    axial_vel = fields[:, 1] / density
    radial_vel = fields[:, 2] / density
    swirl_vel = fields[:, 3] / density
    kinetic = fields[:, 1] * axial_vel + fields[:, 2] * radial_vel + fields[:, 3] * swirl_vel
    pressure = GAS_FACTOR * (fields[:, 4] - 0.5 * kinetic)
    return axial_vel, radial_vel, swirl_vel, pressure


def axial_flux(fields):
    axial_vel, radial_vel, swirl_vel, pressure = velocities(fields)
    return jnp.stack([fields[:, 1], fields[:, 1] * axial_vel + pressure, fields[:, 2] * axial_vel,
                      fields[:, 3] * axial_vel, axial_vel * (fields[:, 4] + pressure)], axis=1)


def radial_flux(fields):
    axial_vel, radial_vel, swirl_vel, pressure = velocities(fields)
    return jnp.stack([fields[:, 2], fields[:, 1] * radial_vel, fields[:, 2] * radial_vel + pressure,
                      fields[:, 3] * radial_vel, radial_vel * (fields[:, 4] + pressure)], axis=1)


def swirl_flux(fields):
    axial_vel, radial_vel, swirl_vel, pressure = velocities(fields)
    return jnp.stack([fields[:, 3], fields[:, 1] * swirl_vel, fields[:, 2] * swirl_vel,
                      fields[:, 3] * swirl_vel + pressure, swirl_vel * (fields[:, 4] + pressure)], axis=1)


def central_difference(values, along, extent):
    result = None
    for offset, weight in zip((1, 2, 3, 4), STENCIL):
        forward_part = lax.slice_in_dim(values, 4 + offset, 4 + offset + extent, axis=along)
        backward_part = lax.slice_in_dim(values, 4 - offset, 4 - offset + extent, axis=along)
        contribution = weight * (forward_part - backward_part)
        result = contribution if result is None else result + contribution
    return result


def section_update(axial_padded, theta_padded, opposite, fields):
    stations = fields.shape[0]
    radial = fields.shape[2]
    width = fields.shape[3]
    axial_term = central_difference(axial_flux(axial_padded), 0, stations)
    flips = jnp.array([1.0, 1.0, -1.0, -1.0, 1.0], jnp.float32).reshape(1, 5, 1, 1)
    mirrored = opposite[:, :, ::-1, :] * flips
    outer_rows = jnp.broadcast_to(fields[:, :, -1:, :], (stations, 5, 4, width))
    radial_padded = jnp.concatenate([mirrored, fields, outer_rows], axis=2)
    signed_radius = (jnp.arange(radial + 8, dtype=jnp.float32) - 3.5).reshape(1, 1, -1, 1)
    radial_term = central_difference(radial_flux(radial_padded) * signed_radius, 2, radial)
    swirl_term = central_difference(swirl_flux(theta_padded), 3, width) * (NT / (2.0 * math.pi))
    axial_vel, radial_vel, swirl_vel, pressure = velocities(fields)
    nothing = jnp.zeros_like(pressure)
    source = jnp.stack([nothing, nothing, fields[:, 3] * swirl_vel + pressure,
                        -fields[:, 2] * swirl_vel, nothing], axis=1)
    radius = (jnp.arange(radial, dtype=jnp.float32) + 0.5).reshape(1, 1, -1, 1)
    tendency = -axial_term - (radial_term + swirl_term - source) / radius
    return fields + TIME_STEP * tendency


def fourier_basis(columns):
    harmonic = jnp.arange(2 * MODE_MOST, dtype=jnp.int32) % MODE_MOST
    product = (columns.astype(jnp.int32)[:, None] * harmonic[None, :]) % NT
    angle = product.astype(jnp.float32) * (2.0 * math.pi / NT)
    cosine_side = (jnp.arange(2 * MODE_MOST, dtype=jnp.int32) < MODE_MOST)[None, :]
    return jnp.where(cosine_side, jnp.cos(angle), jnp.sin(angle)).astype(jnp.float32)


def mode_weights(cycle_modes):
    harmonic = jnp.arange(2 * MODE_MOST, dtype=jnp.int32) % MODE_MOST
    base_weight = jnp.where(harmonic == 0, 1.0 / NT, 2.0 / NT).astype(jnp.float32)
    keep = harmonic[None, :] < cycle_modes[:, None]
    return jnp.where(keep, base_weight[None, :], 0.0).astype(jnp.float32)


def reference(conserved, cycle_modes, filtered_cycles):
    stations = conserved.shape[0]
    block = 8 if stations % 8 == 0 else 1
    basis = fourier_basis(jnp.arange(NT, dtype=jnp.int32))
    kept_weights = mode_weights(cycle_modes)
    cycle_ids = jnp.arange(NRF, dtype=jnp.int32)

    def one_block(first_row):
        rows = jnp.clip(first_row - 4 + jnp.arange(block + 8, dtype=jnp.int32), 0, stations - 1)
        axial_padded = jnp.take(conserved, rows, axis=0)
        center = lax.dynamic_slice_in_dim(conserved, first_row, block, 0)
        theta_padded = jnp.concatenate([center[..., -4:], center, center[..., :4]], axis=3)
        opposite = jnp.roll(center[:, :, :4, :], NT // 2, axis=3)
        section = section_update(axial_padded, theta_padded, opposite, center)
        inner_cycles = section[:, :, :NRF, :]
        coefficients = jnp.einsum("afrt,tc->afrc", inner_cycles, basis, precision=lax.Precision.HIGHEST)
        smoothed = jnp.einsum("afrc,tc->afrt", coefficients * kept_weights[None, None], basis,
                              precision=lax.Precision.HIGHEST)
        counts = lax.dynamic_slice_in_dim(filtered_cycles, first_row, block, 0)
        chosen = jnp.where(cycle_ids[None, None, :, None] < counts[:, None, None, None], smoothed, inner_cycles)
        return jnp.concatenate([chosen, section[:, :, NRF:, :]], axis=2)

    firsts = jnp.arange(0, stations, block, dtype=jnp.int32)
    blocks = lax.map(one_block, firsts)
    return blocks.reshape(conserved.shape)
```

```python
import functools
import math

import jax
import jax.numpy as jnp
import numpy as np
from jax import lax
from jax.experimental import pallas as pl
from jax.experimental.pallas import tpu as pltpu
from jax.sharding import PartitionSpec as P

MODE_MOST = 64
STENCIL = (0.8, -0.2, 4.0 / 105.0, -1.0 / 280.0)
REACH = len(STENCIL)
GAS_FACTOR = 0.4
TIME_STEP = 0.1
COMPONENTS = 5
TILE = 8
LANES = 128
CHUNKS = ((0, 2), (2, 1), (3, 1))

VMEM = pl.BlockSpec(memory_space=pltpu.VMEM)
SMEM = pl.BlockSpec(memory_space=pltpu.SMEM)
ANY = pl.BlockSpec(memory_space=pl.ANY)
PARAMS = dict(vmem_limit_bytes=8 << 20)


def primitives(s):
    inverse = 1.0 / s[0]
    a, b, c = s[1] * inverse, s[2] * inverse, s[3] * inverse
    p = GAS_FACTOR * (s[4] - 0.5 * (s[1] * a + s[2] * b + s[3] * c))
    return a, b, c, p


def flux(s, vel, p, along):
    out = [s[along]] + [s[i] * vel for i in (1, 2, 3)] + [vel * (s[4] + p)]
    out[along] = out[along] + p
    return out


def axial_flux(s):
    inverse = 1.0 / s[0]
    a = s[1] * inverse
    p = GAS_FACTOR * (s[4] - 0.5 * ((s[1] * s[1] + s[2] * s[2] + s[3] * s[3]) * inverse))
    return flux(s, a, p, 1)


def halo_terms(x_ref, stores, base, step, forward, rows):
    scale = jnp.where(forward, -TIME_STEP, TIME_STEP)
    for r in range(0, rows, TILE):
        near = []
        for h in range(REACH):
            at = base + step * h
            near.append(axial_flux([x_ref[at, c, r : r + TILE, :] for c in range(COMPONENTS)]))
        for i in range(REACH):
            for c in range(COMPONENTS):
                total = None
                for h in range(i + 1):
                    part = STENCIL[REACH + h - i - 1] * near[h][c]
                    total = part if total is None else total + part
                stores(i, c, r, scale * total)


def outer_kernel(last, x_ref, t_ref):
    me = lax.axis_index("ax")
    even = lax.rem(me, 2) == 0
    end = (me == 0) | (me == last)
    base = jnp.where(even, 0, REACH - 1)
    step = jnp.where(end, 0, jnp.where(even, 1, -1))
    forward = even != end

    def store(i, c, r, value):
        t_ref[jnp.where(forward, i, REACH - 1 - i), c, r : r + TILE, :] = value

    halo_terms(x_ref, store, base, step, forward, x_ref.shape[2])


def inner_kernel(x_ref, t_ref, pack_ref):
    me = lax.axis_index("ax")
    forward = lax.rem(me, 2) == 1
    base = jnp.where(forward, 0, REACH - 1)
    step = jnp.where(forward, 1, -1)
    stations, _, rows, width = x_ref.shape

    def store(i, c, r, value):
        t_ref[jnp.where(forward, i, REACH - 1 - i), c, r : r + TILE, :] = value

    halo_terms(x_ref, store, base, step, forward, rows)
    groups = rows // TILE
    lane = lax.broadcasted_iota(jnp.int32, (TILE, LANES), 1)
    for c in range(COMPONENTS):
        edge = jnp.zeros((TILE, LANES), jnp.float32)
        for s in range(stations):
            pack_ref[c, s * REACH : (s + 1) * REACH, :] = x_ref[s, c, 0:REACH, :]
            for g in range(groups):
                place = (s * groups + g) * 2 * REACH
                first = x_ref[s, c, g * TILE : (g + 1) * TILE, 0:LANES]
                final = x_ref[s, c, g * TILE : (g + 1) * TILE, width - LANES : width]
                both = pltpu.roll(jnp.where(lane < REACH, first, final), (place + REACH) % LANES, 1)
                edge = jnp.where((lane >= place) & (lane < place + 2 * REACH), both, edge)
        pack_ref[c, stations * REACH : stations * REACH + TILE, 0:LANES] = edge
        if width > LANES:
            pack_ref[c, stations * REACH : stations * REACH + TILE, LANES:width] = jnp.zeros(
                (TILE, width - LANES), jnp.float32
            )


def base_kernel(
    turn, x_ref, inner_ref, own_ref, left_ref, right_ref, across_ref, modes_ref,
    base_ref, weight_ref, scratch,
):
    stations, _, rows, width = x_ref.shape
    points = int(round(turn))
    groups = rows // TILE
    lane = lax.broadcasted_iota(jnp.int32, (TILE, LANES), 1)
    edge_rows = pl.ds(stations * REACH, TILE)
    per_angle = turn / (2.0 * math.pi)

    slot = lane % (2 * REACH)
    from_left = slot < REACH

    def edge_flux(s):
        _, _, vel, p = primitives(s)
        return flux(s, vel, p, 3)

    own = edge_flux([own_ref[c, edge_rows, 0:LANES] for c in range(COMPONENTS)])
    other = edge_flux(
        [
            jnp.where(from_left, left_ref[c, edge_rows, 0:LANES], right_ref[c, edge_rows, 0:LANES])
            for c in range(COMPONENTS)
        ]
    )
    fixes = []
    for c in range(COMPONENTS):
        change = other[c] - own[c]
        fix = jnp.zeros((TILE, LANES), jnp.float32)
        for k in range(1, REACH + 1):
            ahead = pltpu.roll(change, LANES - k, 1)
            behind = pltpu.roll(change, k, 1)
            fix = fix + STENCIL[k - 1] * jnp.where(
                from_left,
                jnp.where(slot + k >= REACH, ahead, 0.0),
                jnp.where(slot - k < REACH, -behind, 0.0),
            )
        fixes.append(fix)

    for s in range(stations):
        cross = [across_ref[c, s * REACH : (s + 1) * REACH, :] for c in range(COMPONENTS)]
        _, vel, _, p = primitives(cross)
        far = flux(cross, vel, p, 2)
        for c in range(COMPONENTS):
            sign = -1.0 if c in (2, 3) else 1.0
            for i in range(REACH):
                scratch[c, TILE - 1 - i : TILE - i, :] = (sign * (i + 0.5)) * far[c][i : i + 1, :]
        for g in range(groups):
            at = slice(g * TILE, (g + 1) * TILE)
            state = [x_ref[s, c, at, :] for c in range(COMPONENTS)]
            _, vel, _, p = primitives(state)
            out = flux(state, vel, p, 2)
            radius = (
                lax.broadcasted_iota(jnp.int32, (TILE, width), 0).astype(jnp.float32) + (g * TILE + 0.5)
            )
            for c in range(COMPONENTS):
                scratch[c, TILE + g * TILE : TILE + (g + 1) * TILE, :] = radius * out[c]
                if g == groups - 1:
                    edge = out[c][TILE - 1 : TILE, :]
                    for m in range(1, REACH + 1):
                        scratch[c, TILE + rows + m - 1 : TILE + rows + m, :] = (rows - 0.5 + m) * edge
        for g in range(groups):
            at = slice(g * TILE, (g + 1) * TILE)
            state = [x_ref[s, c, at, :] for c in range(COMPONENTS)]
            _, _, vel, p = primitives(state)
            swirl = flux(state, vel, p, 3)
            radius = (
                lax.broadcasted_iota(jnp.int32, (TILE, width), 0).astype(jnp.float32) + (g * TILE + 0.5)
            )
            scale = TIME_STEP / radius
            place = (s * groups + g) * 2 * REACH
            source = {2: state[3] * vel + p, 3: -(state[2] * vel)}
            for c in range(COMPONENTS):
                turned = None
                radial = None
                for k in range(1, REACH + 1):
                    part = STENCIL[k - 1] * (
                        pltpu.roll(swirl[c], width - k, 1) - pltpu.roll(swirl[c], k, 1)
                    )
                    turned = part if turned is None else turned + part
                    start = TILE + g * TILE
                    part = STENCIL[k - 1] * (
                        scratch[c, start + k : start + k + TILE, :]
                        - scratch[c, start - k : start - k + TILE, :]
                    )
                    radial = part if radial is None else radial + part
                fix = pltpu.roll(fixes[c], (LANES - REACH - place) % LANES, 1)
                head = jnp.where(lane < REACH, fix, 0.0)
                tail = jnp.where(lane >= LANES - REACH, fix, 0.0)
                if width == LANES:
                    turned = turned + (head + tail)
                else:
                    middle = [jnp.zeros((TILE, width - 2 * LANES), jnp.float32)] if width > 2 * LANES else []
                    turned = turned + jnp.concatenate([head] + middle + [tail], axis=1)
                total = radial + per_angle * turned
                if c in source:
                    total = total - source[c]
                base_ref[s, c, at, :] = state[c] + inner_ref[s, c, at, :] - scale * total

    for r in range(0, rows, TILE):
        near = [
            axial_flux([x_ref[h, c, r : r + TILE, :] for c in range(COMPONENTS)]) for h in range(stations)
        ]
        for s in range(stations):
            for c in range(COMPONENTS):
                total = None
                for h in range(stations):
                    if h == s:
                        continue
                    weight = STENCIL[abs(h - s) - 1] * (-TIME_STEP if h > s else TIME_STEP)
                    part = weight * near[h][c]
                    total = part if total is None else total + part
                base_ref[s, c, r : r + TILE, :] += total

    columns = 2 * MODE_MOST
    harmonic = lax.broadcasted_iota(jnp.int32, (rows, columns), 1) % MODE_MOST
    row = lax.broadcasted_iota(jnp.int32, (rows, columns), 0)
    kept = jnp.zeros((rows, columns), jnp.int32)
    for j in range(rows):
        kept = jnp.where(row == j, modes_ref[j], kept)
    weight = jnp.where(harmonic == 0, 1.0 / points, 2.0 / points).astype(jnp.float32)
    weight_ref[...] = jnp.where(harmonic < kept, weight, 0.0)


def forward_kernel(first, count, base_ref, t_ref, basis_ref, section_ref, coeff_ref):
    section = base_ref[first : first + count] + t_ref[...]
    section_ref[...] = section
    lines = section.reshape(-1, section.shape[-1])
    basis = basis_ref[lax.axis_index("az")]
    coeff_ref[...] = lax.dot_general(
        lines, basis, (((1,), (0,)), ((), ())),
        precision=lax.Precision.HIGHEST, preferred_element_type=jnp.float32,
    )


def inverse_kernel(first, count, section_ref, mine_ref, other_ref, weight_ref, basis_ref, limit_ref, *rest):
    out_ref, buffer, sem = rest[-3:]
    _, _, rows, width = section_ref.shape
    basis = basis_ref[lax.axis_index("az")]
    lines = COMPONENTS * rows
    weight = weight_ref[...]
    row = lax.broadcasted_iota(jnp.int32, (rows, width), 0)
    copies = []
    for s in range(count):
        part = pl.ds(s * lines, lines)
        total = mine_ref[part, :] + other_ref[part, :]
        total = (total.reshape(COMPONENTS, rows, -1) * weight[None]).reshape(lines, -1)
        smooth = lax.dot_general(
            total, basis, (((1,), (1,)), ((), ())),
            precision=lax.Precision.HIGHEST, preferred_element_type=jnp.float32,
        ).reshape(COMPONENTS, rows, width)
        inside = (row < limit_ref[first + s])[None]
        buffer[s] = jnp.where(inside, smooth, section_ref[s])
        copy = pltpu.make_async_copy(buffer.at[s], out_ref.at[first + s], sem.at[s])
        copy.start()
        copies.append(copy)
    for copy in copies:
        copy.wait()


def fourier_tables(sectors, width):
    points = sectors * width
    harmonic = np.arange(2 * MODE_MOST) % MODE_MOST
    angle = (np.arange(points)[:, None] * harmonic[None, :] % points) * (2.0 * np.pi / points)
    table = np.where(np.arange(2 * MODE_MOST)[None, :] < MODE_MOST, np.cos(angle), np.sin(angle))
    return table.astype(np.float32).reshape(sectors, width, 2 * MODE_MOST)


def per_device(conserved, cycle_modes, filtered_cycles):
    line = lax.axis_size("ax")
    sectors = lax.axis_size("az")
    stations, components, rows, width = conserved.shape
    if stations != REACH or components != COMPONENTS or line % 2 or sectors % 2:
        raise ValueError("unsupported shape")
    if (stations * rows // TILE) * 2 * REACH > LANES or width % LANES or rows % TILE:
        raise ValueError("unsupported shape")
    block = jax.ShapeDtypeStruct(conserved.shape, jnp.float32)
    params = pltpu.CompilerParams(**PARAMS)

    terms = pl.pallas_call(
        functools.partial(outer_kernel, line - 1),
        out_shape=block, in_specs=[VMEM], out_specs=VMEM, compiler_params=params, name="outer",
    )(conserved)
    ends = [(0, 0), (line - 1, line - 1)]
    pairs = [(i, i + 1) for i in range(1, line - 1, 2)]
    outer_route = ends + pairs + [(j, i) for i, j in pairs]
    outer = [
        lax.ppermute(lax.slice_in_dim(terms, a, a + n, axis=0), "ax", outer_route) for a, n in CHUNKS
    ]
    inner, pack = pl.pallas_call(
        inner_kernel,
        out_shape=(block, jax.ShapeDtypeStruct((COMPONENTS, stations * REACH + TILE, width), jnp.float32)),
        in_specs=[VMEM], out_specs=(VMEM, VMEM), compiler_params=params, name="inner",
    )(conserved)
    inner = lax.ppermute(inner, "ax", [(i, i ^ 1) for i in range(line)])

    def turned(value, by):
        return lax.ppermute(value, "az", [(i, (i + by) % sectors) for i in range(sectors)])

    across = turned(pack, sectors // 2)
    left, right = (across, across) if sectors == 2 else (turned(pack, 1), turned(pack, -1))
    base, weight = pl.pallas_call(
        functools.partial(base_kernel, float(width * sectors)),
        out_shape=(block, jax.ShapeDtypeStruct((rows, 2 * MODE_MOST), jnp.float32)),
        in_specs=[VMEM] * 6 + [SMEM], out_specs=(VMEM, VMEM),
        scratch_shapes=[pltpu.VMEM((COMPONENTS, rows + 2 * TILE, width), jnp.float32)],
        compiler_params=params, name="base",
    )(conserved, inner, pack, left, right, across, cycle_modes)
    basis = jnp.asarray(fourier_tables(sectors, width))
    out = None
    for (first, count), arrived in zip(CHUNKS, outer):
        section, mine = pl.pallas_call(
            functools.partial(forward_kernel, first, count),
            out_shape=(
                jax.ShapeDtypeStruct((count,) + conserved.shape[1:], jnp.float32),
                jax.ShapeDtypeStruct((count * components * rows, 2 * MODE_MOST), jnp.float32),
            ),
            in_specs=[VMEM] * 3, out_specs=(VMEM, VMEM), compiler_params=params, name="forward%d" % first,
        )(base, arrived, basis)
        other = turned(mine, 1) if sectors == 2 else lax.psum(mine, "az") - mine
        more = () if out is None else (out,)
        out = pl.pallas_call(
            functools.partial(inverse_kernel, first, count),
            out_shape=block,
            in_specs=[VMEM] * 5 + [SMEM] + [ANY] * len(more), out_specs=ANY,
            scratch_shapes=[
                pltpu.VMEM((count,) + conserved.shape[1:], jnp.float32),
                pltpu.SemaphoreType.DMA((count,)),
            ],
            input_output_aliases={6: 0} if more else {},
            compiler_params=params, name="inverse%d" % first,
        )(section, mine, other, weight, basis, filtered_cycles, *more)
    return out


def solution(mesh):
    placed = (P("ax", None, None, "az"), P(), P("ax"))
    return jax.shard_map(
        per_device, mesh=mesh, in_specs=placed, out_specs=P("ax", None, None, "az"), check_vma=False
    )
```

```python
import functools
import math

import jax
import jax.numpy as jnp
import numpy as np
from jax import lax
from jax.experimental import pallas as pl
from jax.experimental.pallas import tpu as pltpu
from jax.sharding import PartitionSpec as P


MODE_MOST = 64
STENCIL = (0.8, -0.2, 4.0 / 105.0, -1.0 / 280.0)
REACH = len(STENCIL)
GAS_FACTOR = 0.4
TIME_STEP = 0.1
COMPONENTS = 5
TILE = 8
LANES = 128
SENDS = ((0, 1), (1, 1), (2, 1), (3, 1))
GROUPS = ((0, 2), (2, 1), (3, 1))
LAST = len(GROUPS) - 1

VMEM = pl.BlockSpec(memory_space=pltpu.VMEM)
SMEM = pl.BlockSpec(memory_space=pltpu.SMEM)
ANY = pl.BlockSpec(memory_space=pl.ANY)
PARAMS = dict(vmem_limit_bytes=8 << 20)


def exact_dot(a, b):
    return lax.dot_general(
        a, b, (((1,), (0,)), ((), ())), precision=lax.Precision.HIGHEST, preferred_element_type=jnp.float32
    )


def primitives(s):
    inverse = 1.0 / s[0]
    a, b, c = s[1] * inverse, s[2] * inverse, s[3] * inverse
    p = GAS_FACTOR * (s[4] - 0.5 * (s[1] * a + s[2] * b + s[3] * c))
    return a, b, c, p


def flux(s, vel, p, along):
    out = [s[along]] + [s[i] * vel for i in (1, 2, 3)] + [vel * (s[4] + p)]
    out[along] = out[along] + p
    return out


def axial_flux(s):
    inverse = 1.0 / s[0]
    a = s[1] * inverse
    p = GAS_FACTOR * (s[4] - 0.5 * ((s[1] * s[1] + s[2] * s[2] + s[3] * s[3]) * inverse))
    return flux(s, a, p, 1)


def halo_terms(x_ref, base, step, forward, chunks, outs):
    rows = x_ref.shape[2]
    scale = jnp.where(forward, -TIME_STEP, TIME_STEP)
    after = [[STENCIL[REACH + h - i - 1] if h <= i else 0.0 for h in range(REACH)] for i in range(REACH)]
    before = [[STENCIL[i + h] if i + h < REACH else 0.0 for h in range(REACH)] for i in range(REACH)]
    for r in range(0, rows, TILE):
        at = slice(r, r + TILE)
        near = []
        for h in range(REACH):
            near.append(axial_flux([x_ref[base + step * h, c, at, :] for c in range(COMPONENTS)]))
        for (first, count), out in zip(chunks, outs):
            for n in range(count):
                i = first + n
                weights = [scale * jnp.where(forward, after[i][h], before[i][h]) for h in range(REACH)]
                for c in range(COMPONENTS):
                    out[n, c, at, :] = sum(w * near[h][c] for h, w in enumerate(weights))


def toward(me, last):
    even = lax.rem(me, 2) == 0
    end = (me == 0) | (me == last)
    base = jnp.where(even, 0, REACH - 1)
    step = jnp.where(end, 0, jnp.where(even, 1, -1))
    return base, step, even != end


def outer_kernel(last, x_ref, *outs):
    base, step, forward = toward(lax.axis_index("ax"), last)
    halo_terms(x_ref, base, step, forward, SENDS, outs)


def inner_kernel(x_ref, t_ref, pack_ref):
    stations, _, rows, width = x_ref.shape
    forward = lax.rem(lax.axis_index("ax"), 2) == 1
    base = jnp.where(forward, 0, REACH - 1)
    step = jnp.where(forward, 1, -1)
    halo_terms(x_ref, base, step, forward, [(0, stations)], [t_ref])
    groups = rows // TILE
    lane = lax.broadcasted_iota(jnp.int32, (TILE, LANES), 1)
    for c in range(COMPONENTS):
        edge = jnp.zeros((TILE, LANES), jnp.float32)
        for s in range(stations):
            pack_ref[c, s * REACH : (s + 1) * REACH, :] = x_ref[s, c, 0:REACH, :]
            for g in range(groups):
                place = (s * groups + g) * 2 * REACH
                first = x_ref[s, c, g * TILE : (g + 1) * TILE, 0:LANES]
                final = x_ref[s, c, g * TILE : (g + 1) * TILE, width - LANES : width]
                both = pltpu.roll(jnp.where(lane < REACH, first, final), (place + REACH) % LANES, 1)
                edge = jnp.where((lane >= place) & (lane < place + 2 * REACH), both, edge)
        pack_ref[c, stations * REACH : stations * REACH + TILE, 0:LANES] = edge
        if width > LANES:
            pack_ref[c, stations * REACH : stations * REACH + TILE, LANES:width] = jnp.zeros(
                (TILE, width - LANES), jnp.float32
            )


def base_kernel(
    turn, x_ref, inner_ref, own_ref, left_ref, right_ref, across_ref, table_ref, back_ref, modes_ref, limit_ref,
    base_ref, weight_ref, inside_ref, basis_ref, unbasis_ref, radial_ref, axial_ref,
):
    stations, _, rows, width = x_ref.shape
    points = int(round(turn))
    groups = rows // TILE
    lane = lax.broadcasted_iota(jnp.int32, (TILE, LANES), 1)
    edge_rows = pl.ds(stations * REACH, TILE)
    per_angle = turn / (2.0 * math.pi)

    slot = lane % (2 * REACH)
    from_left = slot < REACH

    def edge_flux(s):
        _, _, vel, p = primitives(s)
        return flux(s, vel, p, 3)

    own = edge_flux([own_ref[c, edge_rows, 0:LANES] for c in range(COMPONENTS)])
    other = edge_flux(
        [
            jnp.where(from_left, left_ref[c, edge_rows, 0:LANES], right_ref[c, edge_rows, 0:LANES])
            for c in range(COMPONENTS)
        ]
    )
    fixes = []
    for c in range(COMPONENTS):
        change = other[c] - own[c]
        fix = jnp.zeros((TILE, LANES), jnp.float32)
        for k in range(1, REACH + 1):
            ahead = pltpu.roll(change, LANES - k, 1)
            behind = pltpu.roll(change, k, 1)
            fix = fix + STENCIL[k - 1] * jnp.where(
                from_left,
                jnp.where(slot + k >= REACH, ahead, 0.0),
                jnp.where(slot - k < REACH, -behind, 0.0),
            )
        fixes.append(fix)

    for s in range(stations):
        cross = [across_ref[c, s * REACH : (s + 1) * REACH, :] for c in range(COMPONENTS)]
        _, vel, _, p = primitives(cross)
        far = flux(cross, vel, p, 2)
        for c in range(COMPONENTS):
            sign = -1.0 if c in (2, 3) else 1.0
            for i in range(REACH):
                radial_ref[s, c, TILE - 1 - i : TILE - i, :] = (sign * (i + 0.5)) * far[c][i : i + 1, :]
        for g in range(groups):
            at = slice(g * TILE, (g + 1) * TILE)
            state = [x_ref[s, c, at, :] for c in range(COMPONENTS)]
            a, b, vel, p = primitives(state)
            ahead = flux(state, a, p, 1)
            out = flux(state, b, p, 2)
            swirl = flux(state, vel, p, 3)
            radius = (
                lax.broadcasted_iota(jnp.int32, (TILE, width), 0).astype(jnp.float32) + (g * TILE + 0.5)
            )
            for c in range(COMPONENTS):
                axial_ref[s, c, at, :] = TIME_STEP * ahead[c]
                radial_ref[s, c, TILE + g * TILE : TILE + (g + 1) * TILE, :] = radius * out[c]
                if g == groups - 1:
                    edge = out[c][TILE - 1 : TILE, :]
                    for m in range(1, REACH + 1):
                        radial_ref[s, c, TILE + rows + m - 1 : TILE + rows + m, :] = (rows - 0.5 + m) * edge
            place = (s * groups + g) * 2 * REACH
            source = {2: state[3] * vel + p, 3: -(state[2] * vel)}
            for c in range(COMPONENTS):
                turned = None
                for k in range(1, REACH + 1):
                    part = STENCIL[k - 1] * (
                        pltpu.roll(swirl[c], width - k, 1) - pltpu.roll(swirl[c], k, 1)
                    )
                    turned = part if turned is None else turned + part
                fix = pltpu.roll(fixes[c], (LANES - REACH - place) % LANES, 1)
                head = jnp.where(lane < REACH, fix, 0.0)
                tail = jnp.where(lane >= LANES - REACH, fix, 0.0)
                if width == LANES:
                    turned = turned + (head + tail)
                else:
                    middle = [jnp.zeros((TILE, width - 2 * LANES), jnp.float32)] if width > 2 * LANES else []
                    turned = turned + jnp.concatenate([head] + middle + [tail], axis=1)
                total = per_angle * turned
                if c in source:
                    total = total - source[c]
                base_ref[s, c, at, :] = total
    for g in range(groups):
        at = slice(g * TILE, (g + 1) * TILE)
        start = TILE + g * TILE
        radius = lax.broadcasted_iota(jnp.int32, (TILE, width), 0).astype(jnp.float32) + (g * TILE + 0.5)
        scale = TIME_STEP / radius
        for c in range(COMPONENTS):
            near = [axial_ref[h, c, at, :] for h in range(stations)]
            for s in range(stations):
                total = base_ref[s, c, at, :]
                for k in range(1, REACH + 1):
                    total = total + STENCIL[k - 1] * (
                        radial_ref[s, c, start + k : start + k + TILE, :]
                        - radial_ref[s, c, start - k : start - k + TILE, :]
                    )
                total = x_ref[s, c, at, :] + inner_ref[s, c, at, :] - scale * total
                for h in range(stations):
                    if h != s:
                        total = total + (STENCIL[abs(h - s) - 1] * (-1.0 if h > s else 1.0)) * near[h]
                base_ref[s, c, at, :] = total

    sector = lax.axis_index("az")
    basis_ref[...] = table_ref[sector]
    unbasis_ref[...] = back_ref[sector]
    line = lax.broadcasted_iota(jnp.int32, (rows, LANES), 0)
    for s in range(stations):
        inside_ref[s] = (line < limit_ref[s]).astype(jnp.float32)
    columns = 2 * MODE_MOST
    harmonic = lax.broadcasted_iota(jnp.int32, (rows, columns), 1) % MODE_MOST
    row = lax.broadcasted_iota(jnp.int32, (rows, columns), 0)
    kept = jnp.zeros((rows, columns), jnp.int32)
    for j in range(rows):
        kept = jnp.where(row == j, modes_ref[j], kept)
    weight = jnp.where(harmonic == 0, 1.0 / points, 2.0 / points).astype(jnp.float32)
    weight_ref[...] = jnp.where(harmonic < kept, weight, 0.0)


def forward_kernel(n, last, base_ref, basis_ref, *refs):
    section_ref, coeff_ref = refs[-2:]
    first, count = GROUPS[n]
    width = base_ref.shape[-1]
    me = lax.axis_index("ax")
    end = (me == 0) | (me == last)
    inside = [(a, m) for a, m in SENDS if first <= a < first + count]
    for i, (a, m) in enumerate(inside):
        terms = jnp.where(end, refs[2 * i][...], refs[2 * i + 1][...])
        section_ref[a - first : a - first + m] = base_ref[a : a + m] + terms
    coeff_ref[...] = exact_dot(section_ref[...].reshape(-1, width), basis_ref[...])


def smooth(total, section, weight, unbasis, inside):
    _, rows, width = section.shape
    kept = (total.reshape(COMPONENTS, rows, -1) * weight[None]).reshape(COMPONENTS * rows, -1)
    value = exact_dot(kept, unbasis).reshape(section.shape)
    pick = (inside > 0.5)[None]
    return [
        jnp.where(pick, value[:, :, t : t + LANES], section[:, :, t : t + LANES]) for t in range(0, width, LANES)
    ]


def inverse_kernel(n, section_ref, mine_ref, other_ref, weight_ref, unbasis_ref, inside_ref, *refs):
    first, count = GROUPS[n]
    copies = []
    if n == LAST:
        done, (out_ref, target, sem) = refs[:LAST], refs[LAST:]
        for i, ref in enumerate(done):
            a, m = GROUPS[i]
            copies.append(pltpu.make_async_copy(ref, out_ref.at[a : a + m], sem.at[i]))
        for copy in copies:
            copy.start()
    else:
        (target,) = refs
    lines = COMPONENTS * section_ref.shape[2]
    for s in range(count):
        part = slice(s * lines, (s + 1) * lines)
        total = mine_ref[part, :] + other_ref[part, :]
        parts = smooth(total, section_ref[s], weight_ref[...], unbasis_ref[...], inside_ref[first + s])
        for i, value in enumerate(parts):
            target[s, :, :, i * LANES : (i + 1) * LANES] = value
    if n == LAST:
        copies.append(pltpu.make_async_copy(target, out_ref.at[first : first + count], sem.at[LAST]))
        copies[-1].start()
        for copy in copies:
            copy.wait()


def fourier_tables(sectors, width):
    points = sectors * width
    harmonic = np.arange(2 * MODE_MOST) % MODE_MOST
    angle = (np.arange(points)[:, None] * harmonic[None, :] % points) * (2.0 * np.pi / points)
    table = np.where(np.arange(2 * MODE_MOST)[None, :] < MODE_MOST, np.cos(angle), np.sin(angle))
    return table.astype(np.float32).reshape(sectors, width, 2 * MODE_MOST)


def per_device_inner(conserved, cycle_modes, filtered_cycles):
    line = lax.axis_size("ax")
    sectors = lax.axis_size("az")
    stations, components, rows, width = conserved.shape
    if stations != REACH or components != COMPONENTS or line % 2 or sectors % 2:
        raise ValueError("unsupported shape")
    if (stations * rows // TILE) * 2 * REACH > LANES or width % LANES or rows % TILE:
        raise ValueError("unsupported shape")
    struct = lambda *shape: jax.ShapeDtypeStruct(shape, jnp.float32)
    block = struct(*conserved.shape)
    params = pltpu.CompilerParams(**PARAMS)
    columns = 2 * MODE_MOST

    def turned(value, by):
        return lax.ppermute(value, "az", [(i, (i + by) % sectors) for i in range(sectors)])

    def others(value):
        return turned(value, 1) if sectors == 2 else lax.psum(value, "az") - value

    def call(kernel, outs, ins, out_specs=None, scratch=(), scalars=0):
        many = isinstance(outs, tuple)
        return pl.pallas_call(
            kernel, out_shape=outs, in_specs=[VMEM] * (len(ins) - scalars) + [SMEM] * scalars,
            out_specs=out_specs or ((VMEM,) * len(outs) if many else VMEM),
            scratch_shapes=scratch, compiler_params=params,
        )(*ins)

    shapes = [struct(count, components, rows, width) for _, count in GROUPS]
    lines = components * rows
    table = fourier_tables(sectors, width)
    forth, back = jnp.asarray(table), jnp.asarray(np.ascontiguousarray(table.transpose(0, 2, 1)))

    pairs = [(i, i + 1) for i in range(1, line - 1, 2)]
    pairs += [(j, i) for i, j in pairs]
    route = [(i * sectors + a, j * sectors + a) for i, j in pairs for a in range(sectors)]
    route += [(i * sectors + a, i * sectors + (a + 1) % sectors) for i in (0, line - 1) for a in range(sectors)]
    terms = call(
        functools.partial(outer_kernel, line - 1),
        tuple(struct(m, components, rows, width) for _, m in SENDS), [conserved],
    )
    inner, pack = call(inner_kernel, (block, struct(components, stations * REACH + TILE, width)), [conserved])
    across = turned(pack, sectors // 2)
    left, right = (across, across) if sectors == 2 else (turned(pack, 1), turned(pack, -1))
    arrived = []
    for value in terms:
        arrived.append(lax.ppermute(value, ("ax", "az"), route))
    inner = lax.ppermute(inner, "ax", [(i, i ^ 1) for i in range(line)])
    base, weight, inside, basis, unbasis = call(
        functools.partial(base_kernel, float(width * sectors)),
        (block, struct(rows, columns), struct(stations, rows, LANES), struct(width, columns), struct(columns, width)),
        [conserved, inner, pack, left, right, across, forth, back, cycle_modes, filtered_cycles],
        scalars=2,
        scratch=[
            pltpu.VMEM((stations, COMPONENTS, rows + 2 * TILE, width), jnp.float32),
            pltpu.VMEM(conserved.shape, jnp.float32),
        ],
    )
    done = []
    for n, (first, count) in enumerate(GROUPS):
        both = []
        for (a, m), own, got in zip(SENDS, terms, arrived):
            if first <= a < first + count:
                both += [own, got]
        section, mine = call(
            functools.partial(forward_kernel, n, line - 1), (shapes[n], struct(count * lines, columns)),
            [base, basis, *both],
        )
        other = others(mine)
        operands = [section, mine, other, weight, unbasis, inside]
        if n < LAST:
            done.append(call(functools.partial(inverse_kernel, n), shapes[n], operands))
    return call(
        functools.partial(inverse_kernel, LAST), block, operands + done, out_specs=ANY,
        scratch=[pltpu.VMEM(shapes[LAST].shape, jnp.float32), pltpu.SemaphoreType.DMA((len(GROUPS),))],
    )


def solution(mesh):
    placed = (P("ax", None, None, "az"), P(), P("ax"))
    return jax.shard_map(
        per_device_inner, mesh=mesh, in_specs=placed, out_specs=P("ax", None, None, "az"), check_vma=False
    )
```

```python
import functools
import math

import jax
import jax.numpy as jnp
import numpy as np
from jax import lax
from jax.experimental import pallas as pl
from jax.experimental.pallas import tpu as pltpu
from jax.sharding import PartitionSpec as P


MODE_MOST = 64
STENCIL = (0.8, -0.2, 4.0 / 105.0, -1.0 / 280.0)
REACH = len(STENCIL)
GAS_FACTOR = 0.4
TIME_STEP = 0.1
COMPONENTS = 5
TILE = 8
LANES = 128
SENDS = ((0, 1), (1, 1), (2, 1), (3, 1))
GROUPS = ((0, 2), (2, 1), (3, 1))
LAST = len(GROUPS) - 1

VMEM = pl.BlockSpec(memory_space=pltpu.VMEM)
SMEM = pl.BlockSpec(memory_space=pltpu.SMEM)
ANY = pl.BlockSpec(memory_space=pl.ANY)
PARAMS = dict(vmem_limit_bytes=8 << 20)


def halves(value):
    high = value.astype(jnp.bfloat16)
    return high, (value - high.astype(jnp.float32)).astype(jnp.bfloat16)


def close_dot(a, high, low):
    def dot(p, q):
        return lax.dot_general(p, q, (((1,), (0,)), ((), ())), preferred_element_type=jnp.float32)

    top, rest = halves(a)
    return dot(top, high) + (dot(top, low) + dot(rest, high))


def primitives(s):
    inverse = 1.0 / s[0]
    a, b, c = s[1] * inverse, s[2] * inverse, s[3] * inverse
    p = GAS_FACTOR * (s[4] - 0.5 * (s[1] * a + s[2] * b + s[3] * c))
    return a, b, c, p


def flux(s, vel, p, along):
    out = [s[along]] + [s[i] * vel for i in (1, 2, 3)] + [vel * (s[4] + p)]
    out[along] = out[along] + p
    return out


def axial_flux(s):
    inverse = 1.0 / s[0]
    a = s[1] * inverse
    p = GAS_FACTOR * (s[4] - 0.5 * ((s[1] * s[1] + s[2] * s[2] + s[3] * s[3]) * inverse))
    return flux(s, a, p, 1)


def halo_terms(x_ref, base, step, forward, chunks, outs):
    rows = x_ref.shape[2]
    scale = jnp.where(forward, -TIME_STEP, TIME_STEP)
    after = [[STENCIL[REACH + h - i - 1] if h <= i else 0.0 for h in range(REACH)] for i in range(REACH)]
    before = [[STENCIL[i + h] if i + h < REACH else 0.0 for h in range(REACH)] for i in range(REACH)]
    for r in range(0, rows, TILE):
        at = slice(r, r + TILE)
        near = []
        for h in range(REACH):
            near.append(axial_flux([x_ref[base + step * h, c, at, :] for c in range(COMPONENTS)]))
        for (first, count), out in zip(chunks, outs):
            for n in range(count):
                i = first + n
                weights = [scale * jnp.where(forward, after[i][h], before[i][h]) for h in range(REACH)]
                for c in range(COMPONENTS):
                    out[n, c, at, :] = sum(w * near[h][c] for h, w in enumerate(weights))


def toward(me, last):
    even = lax.rem(me, 2) == 0
    end = (me == 0) | (me == last)
    base = jnp.where(even, 0, REACH - 1)
    step = jnp.where(end, 0, jnp.where(even, 1, -1))
    return base, step, even != end


def outer_kernel(last, chunks, x_ref, *outs):
    base, step, forward = toward(lax.axis_index("ax"), last)
    halo_terms(x_ref, base, step, forward, chunks, outs)


def inner_kernel(x_ref, t_ref, pack_ref):
    stations, _, rows, width = x_ref.shape
    forward = lax.rem(lax.axis_index("ax"), 2) == 1
    base = jnp.where(forward, 0, REACH - 1)
    step = jnp.where(forward, 1, -1)
    halo_terms(x_ref, base, step, forward, [(0, stations)], [t_ref])
    groups = rows // TILE
    lane = lax.broadcasted_iota(jnp.int32, (TILE, LANES), 1)
    for c in range(COMPONENTS):
        edge = jnp.zeros((TILE, LANES), jnp.float32)
        for s in range(stations):
            pack_ref[c, s * REACH : (s + 1) * REACH, :] = x_ref[s, c, 0:REACH, :]
            for g in range(groups):
                place = (s * groups + g) * 2 * REACH
                first = x_ref[s, c, g * TILE : (g + 1) * TILE, 0:LANES]
                final = x_ref[s, c, g * TILE : (g + 1) * TILE, width - LANES : width]
                both = pltpu.roll(jnp.where(lane < REACH, first, final), (place + REACH) % LANES, 1)
                edge = jnp.where((lane >= place) & (lane < place + 2 * REACH), both, edge)
        pack_ref[c, stations * REACH : stations * REACH + TILE, 0:LANES] = edge
        if width > LANES:
            pack_ref[c, stations * REACH : stations * REACH + TILE, LANES:width] = jnp.zeros(
                (TILE, width - LANES), jnp.float32
            )


def base_kernel(
    turn, x_ref, inner_ref, own_ref, left_ref, right_ref, across_ref, table_ref, back_ref, modes_ref, limit_ref,
    base_ref, weight_ref, inside_ref, basis_ref, unbasis_ref, radial_ref, axial_ref,
):
    stations, _, rows, width = x_ref.shape
    points = int(round(turn))
    groups = rows // TILE
    lane = lax.broadcasted_iota(jnp.int32, (TILE, LANES), 1)
    edge_rows = pl.ds(stations * REACH, TILE)
    per_angle = turn / (2.0 * math.pi)

    slot = lane % (2 * REACH)
    from_left = slot < REACH

    def edge_flux(s):
        _, _, vel, p = primitives(s)
        return flux(s, vel, p, 3)

    own = edge_flux([own_ref[c, edge_rows, 0:LANES] for c in range(COMPONENTS)])
    other = edge_flux(
        [
            jnp.where(from_left, left_ref[c, edge_rows, 0:LANES], right_ref[c, edge_rows, 0:LANES])
            for c in range(COMPONENTS)
        ]
    )
    fixes = []
    for c in range(COMPONENTS):
        change = other[c] - own[c]
        fix = jnp.zeros((TILE, LANES), jnp.float32)
        for k in range(1, REACH + 1):
            ahead = pltpu.roll(change, LANES - k, 1)
            behind = pltpu.roll(change, k, 1)
            fix = fix + STENCIL[k - 1] * jnp.where(
                from_left,
                jnp.where(slot + k >= REACH, ahead, 0.0),
                jnp.where(slot - k < REACH, -behind, 0.0),
            )
        fixes.append(fix)

    for s in range(stations):
        cross = [across_ref[c, s * REACH : (s + 1) * REACH, :] for c in range(COMPONENTS)]
        _, vel, _, p = primitives(cross)
        far = flux(cross, vel, p, 2)
        for c in range(COMPONENTS):
            sign = -1.0 if c in (2, 3) else 1.0
            for i in range(REACH):
                radial_ref[s, c, TILE - 1 - i : TILE - i, :] = (sign * (i + 0.5)) * far[c][i : i + 1, :]
        for g in range(groups):
            at = slice(g * TILE, (g + 1) * TILE)
            state = [x_ref[s, c, at, :] for c in range(COMPONENTS)]
            a, b, vel, p = primitives(state)
            ahead = flux(state, a, p, 1)
            out = flux(state, b, p, 2)
            swirl = flux(state, vel, p, 3)
            radius = (
                lax.broadcasted_iota(jnp.int32, (TILE, width), 0).astype(jnp.float32) + (g * TILE + 0.5)
            )
            for c in range(COMPONENTS):
                axial_ref[s, c, at, :] = TIME_STEP * ahead[c]
                radial_ref[s, c, TILE + g * TILE : TILE + (g + 1) * TILE, :] = radius * out[c]
                if g == groups - 1:
                    edge = out[c][TILE - 1 : TILE, :]
                    for m in range(1, REACH + 1):
                        radial_ref[s, c, TILE + rows + m - 1 : TILE + rows + m, :] = (rows - 0.5 + m) * edge
            place = (s * groups + g) * 2 * REACH
            source = {2: state[3] * vel + p, 3: -(state[2] * vel)}
            for c in range(COMPONENTS):
                turned = None
                for k in range(1, REACH + 1):
                    part = STENCIL[k - 1] * (
                        pltpu.roll(swirl[c], width - k, 1) - pltpu.roll(swirl[c], k, 1)
                    )
                    turned = part if turned is None else turned + part
                fix = pltpu.roll(fixes[c], (LANES - REACH - place) % LANES, 1)
                head = jnp.where(lane < REACH, fix, 0.0)
                tail = jnp.where(lane >= LANES - REACH, fix, 0.0)
                if width == LANES:
                    turned = turned + (head + tail)
                else:
                    middle = [jnp.zeros((TILE, width - 2 * LANES), jnp.float32)] if width > 2 * LANES else []
                    turned = turned + jnp.concatenate([head] + middle + [tail], axis=1)
                total = per_angle * turned
                if c in source:
                    total = total - source[c]
                base_ref[s, c, at, :] = total
    for g in range(groups):
        at = slice(g * TILE, (g + 1) * TILE)
        start = TILE + g * TILE
        radius = lax.broadcasted_iota(jnp.int32, (TILE, width), 0).astype(jnp.float32) + (g * TILE + 0.5)
        scale = TIME_STEP / radius
        for c in range(COMPONENTS):
            near = [axial_ref[h, c, at, :] for h in range(stations)]
            for s in range(stations):
                total = base_ref[s, c, at, :]
                for k in range(1, REACH + 1):
                    total = total + STENCIL[k - 1] * (
                        radial_ref[s, c, start + k : start + k + TILE, :]
                        - radial_ref[s, c, start - k : start - k + TILE, :]
                    )
                total = x_ref[s, c, at, :] + inner_ref[s, c, at, :] - scale * total
                for h in range(stations):
                    if h != s:
                        total = total + (STENCIL[abs(h - s) - 1] * (-1.0 if h > s else 1.0)) * near[h]
                base_ref[s, c, at, :] = total

    sector = lax.axis_index("az")
    basis_ref[0], basis_ref[1] = halves(table_ref[sector])
    unbasis_ref[0], unbasis_ref[1] = halves(back_ref[sector])
    line = lax.broadcasted_iota(jnp.int32, (rows, LANES), 0)
    for s in range(stations):
        inside_ref[s] = (line < limit_ref[s]).astype(jnp.float32)
    columns = 2 * MODE_MOST
    harmonic = lax.broadcasted_iota(jnp.int32, (rows, columns), 1) % MODE_MOST
    row = lax.broadcasted_iota(jnp.int32, (rows, columns), 0)
    kept = jnp.zeros((rows, columns), jnp.int32)
    for j in range(rows):
        kept = jnp.where(row == j, modes_ref[j], kept)
    weight = jnp.where(harmonic == 0, 1.0 / points, 2.0 / points).astype(jnp.float32)
    weight_ref[...] = jnp.where(harmonic < kept, weight, 0.0)


def forward_kernel(n, last, base_ref, basis_ref, *refs):
    section_ref, coeff_ref = refs[-2:]
    first, count = GROUPS[n]
    width = base_ref.shape[-1]
    me = lax.axis_index("ax")
    end = (me == 0) | (me == last)
    inside = [(a, m) for a, m in SENDS if first <= a < first + count]
    for i, (a, m) in enumerate(inside):
        terms = jnp.where(end, refs[2 * i][...], refs[2 * i + 1][...])
        section_ref[a - first : a - first + m] = base_ref[a : a + m] + terms
    coeff_ref[...] = close_dot(section_ref[...].reshape(-1, width), basis_ref[0], basis_ref[1])


def smooth(total, section, weight, unbasis, inside):
    _, rows, width = section.shape
    kept = (total.reshape(COMPONENTS, rows, -1) * weight[None]).reshape(COMPONENTS * rows, -1)
    value = close_dot(kept, unbasis[0], unbasis[1]).reshape(section.shape)
    pick = (inside > 0.5)[None]
    return [
        jnp.where(pick, value[:, :, t : t + LANES], section[:, :, t : t + LANES]) for t in range(0, width, LANES)
    ]


def inverse_kernel(n, section_ref, mine_ref, other_ref, weight_ref, unbasis_ref, inside_ref, *refs):
    first, count = GROUPS[n]
    copies = []
    if n == LAST:
        done, (out_ref, target, sem) = refs[:LAST], refs[LAST:]
        for i, ref in enumerate(done):
            a, m = GROUPS[i]
            copies.append(pltpu.make_async_copy(ref, out_ref.at[a : a + m], sem.at[i]))
        for copy in copies:
            copy.start()
    else:
        (target,) = refs
    lines = COMPONENTS * section_ref.shape[2]
    for s in range(count):
        part = slice(s * lines, (s + 1) * lines)
        total = mine_ref[part, :] + other_ref[part, :]
        parts = smooth(total, section_ref[s], weight_ref[...], unbasis_ref[...], inside_ref[first + s])
        for i, value in enumerate(parts):
            target[s, :, :, i * LANES : (i + 1) * LANES] = value
    if n == LAST:
        copies.append(pltpu.make_async_copy(target, out_ref.at[first : first + count], sem.at[LAST]))
        copies[-1].start()
        for copy in copies:
            copy.wait()


def fourier_tables(sectors, width):
    points = sectors * width
    harmonic = np.arange(2 * MODE_MOST) % MODE_MOST
    angle = (np.arange(points)[:, None] * harmonic[None, :] % points) * (2.0 * np.pi / points)
    table = np.where(np.arange(2 * MODE_MOST)[None, :] < MODE_MOST, np.cos(angle), np.sin(angle))
    return table.astype(np.float32).reshape(sectors, width, 2 * MODE_MOST)


def per_device_inner(conserved, cycle_modes, filtered_cycles):
    line = lax.axis_size("ax")
    sectors = lax.axis_size("az")
    stations, components, rows, width = conserved.shape
    if stations != REACH or components != COMPONENTS or line % 2 or sectors % 2:
        raise ValueError("unsupported shape")
    if (stations * rows // TILE) * 2 * REACH > LANES or width % LANES or rows % TILE:
        raise ValueError("unsupported shape")
    struct = lambda *shape: jax.ShapeDtypeStruct(shape, jnp.float32)
    block = struct(*conserved.shape)
    params = pltpu.CompilerParams(**PARAMS)
    columns = 2 * MODE_MOST

    def turned(value, by):
        return lax.ppermute(value, "az", [(i, (i + by) % sectors) for i in range(sectors)])

    def others(value):
        return turned(value, 1) if sectors == 2 else lax.psum(value, "az") - value

    def call(kernel, outs, ins, out_specs=None, scratch=(), scalars=0):
        many = isinstance(outs, tuple)
        return pl.pallas_call(
            kernel, out_shape=outs, in_specs=[VMEM] * (len(ins) - scalars) + [SMEM] * scalars,
            out_specs=out_specs or ((VMEM,) * len(outs) if many else VMEM),
            scratch_shapes=scratch, compiler_params=params,
        )(*ins)

    shapes = [struct(count, components, rows, width) for _, count in GROUPS]
    lines = components * rows
    table = fourier_tables(sectors, width)
    forth, back = jnp.asarray(table), jnp.asarray(np.ascontiguousarray(table.transpose(0, 2, 1)))

    pairs = [(i, i + 1) for i in range(1, line - 1, 2)]
    pairs += [(j, i) for i, j in pairs]
    route = [(i * sectors + a, j * sectors + a) for i, j in pairs for a in range(sectors)]
    route += [(i * sectors + a, i * sectors + (a + 1) % sectors) for i in (0, line - 1) for a in range(sectors)]
    terms = []
    for chunks in (SENDS[:1], SENDS[1:]):
        terms += call(
            functools.partial(outer_kernel, line - 1, chunks),
            tuple(struct(m, components, rows, width) for _, m in chunks), [conserved],
        )
    inner, pack = call(inner_kernel, (block, struct(components, stations * REACH + TILE, width)), [conserved])
    across = turned(pack, sectors // 2)
    left, right = (across, across) if sectors == 2 else (turned(pack, 1), turned(pack, -1))
    arrived = []
    for value in terms:
        arrived.append(lax.ppermute(value, ("ax", "az"), route))
    inner = lax.ppermute(inner, "ax", [(i, i ^ 1) for i in range(line)])
    base, weight, inside, basis, unbasis = call(
        functools.partial(base_kernel, float(width * sectors)),
        (
            block, struct(rows, columns), struct(stations, rows, LANES),
            jax.ShapeDtypeStruct((2, width, columns), jnp.bfloat16),
            jax.ShapeDtypeStruct((2, columns, width), jnp.bfloat16),
        ),
        [conserved, inner, pack, left, right, across, forth, back, cycle_modes, filtered_cycles],
        scalars=2,
        scratch=[
            pltpu.VMEM((stations, COMPONENTS, rows + 2 * TILE, width), jnp.float32),
            pltpu.VMEM(conserved.shape, jnp.float32),
        ],
    )
    done = []
    for n, (first, count) in enumerate(GROUPS):
        both = []
        for (a, m), own, got in zip(SENDS, terms, arrived):
            if first <= a < first + count:
                both += [own, got]
        section, mine = call(
            functools.partial(forward_kernel, n, line - 1), (shapes[n], struct(count * lines, columns)),
            [base, basis, *both],
        )
        other = others(mine)
        operands = [section, mine, other, weight, unbasis, inside]
        if n < LAST:
            done.append(call(functools.partial(inverse_kernel, n), shapes[n], operands))
    return call(
        functools.partial(inverse_kernel, LAST), block, operands + done, out_specs=ANY,
        scratch=[pltpu.VMEM(shapes[LAST].shape, jnp.float32), pltpu.SemaphoreType.DMA((len(GROUPS),))],
    )


def solution(mesh):
    placed = (P("ax", None, None, "az"), P(), P("ax"))
    return jax.shard_map(
        per_device_inner, mesh=mesh, in_specs=placed, out_specs=P("ax", None, None, "az"), check_vma=False
    )
```

```python
import functools
import math

import jax
import jax.numpy as jnp
import numpy as np
from jax import lax
from jax.experimental import pallas as pl
from jax.experimental.pallas import tpu as pltpu
from jax.sharding import PartitionSpec as P


MODE_MOST = 64
STENCIL = (0.8, -0.2, 4.0 / 105.0, -1.0 / 280.0)
REACH = len(STENCIL)
GAS_FACTOR = 0.4
TIME_STEP = 0.1
COMPONENTS = 5
TILE = 8
LANES = 128
SENDS = ((0, 1), (1, 1), (2, 1), (3, 1))
GROUPS = ((0, 2), (2, 1), (3, 1))
LAST = len(GROUPS) - 1

VMEM = pl.BlockSpec(memory_space=pltpu.VMEM)
SMEM = pl.BlockSpec(memory_space=pltpu.SMEM)
ANY = pl.BlockSpec(memory_space=pl.ANY)
PARAMS = dict(vmem_limit_bytes=8 << 20)


def halves(value):
    high = value.astype(jnp.bfloat16)
    return high, (value - high.astype(jnp.float32)).astype(jnp.bfloat16)


def close_dot(a, high, low):
    def dot(p, q):
        return lax.dot_general(p, q, (((1,), (0,)), ((), ())), preferred_element_type=jnp.float32)

    top, rest = halves(a)
    return dot(top, high) + (dot(top, low) + dot(rest, high))


def primitives(s):
    inverse = 1.0 / s[0]
    a, b, c = s[1] * inverse, s[2] * inverse, s[3] * inverse
    p = GAS_FACTOR * (s[4] - 0.5 * (s[1] * a + s[2] * b + s[3] * c))
    return a, b, c, p


def flux(s, vel, p, along):
    out = [s[along]] + [s[i] * vel for i in (1, 2, 3)] + [vel * (s[4] + p)]
    out[along] = out[along] + p
    return out


def axial_flux(s):
    inverse = 1.0 / s[0]
    a = s[1] * inverse
    p = GAS_FACTOR * (s[4] - 0.5 * ((s[1] * s[1] + s[2] * s[2] + s[3] * s[3]) * inverse))
    return flux(s, a, p, 1)


def halo_terms(x_ref, base, step, forward, chunks, outs):
    rows = x_ref.shape[2]
    scale = jnp.where(forward, -TIME_STEP, TIME_STEP)
    after = [[STENCIL[REACH + h - i - 1] if h <= i else 0.0 for h in range(REACH)] for i in range(REACH)]
    before = [[STENCIL[i + h] if i + h < REACH else 0.0 for h in range(REACH)] for i in range(REACH)]
    for r in range(0, rows, TILE):
        at = slice(r, r + TILE)
        near = []
        for h in range(REACH):
            near.append(axial_flux([x_ref[base + step * h, c, at, :] for c in range(COMPONENTS)]))
        for (first, count), out in zip(chunks, outs):
            for n in range(count):
                i = first + n
                weights = [scale * jnp.where(forward, after[i][h], before[i][h]) for h in range(REACH)]
                for c in range(COMPONENTS):
                    out[n, c, at, :] = sum(w * near[h][c] for h, w in enumerate(weights))


def toward(me, last):
    even = lax.rem(me, 2) == 0
    end = (me == 0) | (me == last)
    base = jnp.where(even, 0, REACH - 1)
    step = jnp.where(end, 0, jnp.where(even, 1, -1))
    return base, step, even != end


def border_terms(near, forward, n, c):
    scale = jnp.where(forward, -TIME_STEP, TIME_STEP)
    return scale * sum(STENCIL[REACH + h - n - 1] * near[h][c] for h in range(n + 1))


def place_of(n):
    return jnp.where(lax.rem(lax.axis_index("ax"), 2) == 0, REACH - 1 - n, n)


def first_kernel(last, x_ref, out_ref, buffer, sem):
    base, _, forward = toward(lax.axis_index("ax"), last)
    copy = pltpu.make_async_copy(x_ref.at[base], buffer, sem)
    copy.start()
    copy.wait()
    for r in range(0, buffer.shape[1], TILE):
        at = slice(r, r + TILE)
        near = [axial_flux([buffer[c, at, :] for c in range(COMPONENTS)])]
        for c in range(COMPONENTS):
            out_ref[0, c, at, :] = border_terms(near, forward, 0, c)


def outer_kernel(last, x_ref, *outs):
    base, step, forward = toward(lax.axis_index("ax"), last)
    for r in range(0, x_ref.shape[2], TILE):
        at = slice(r, r + TILE)
        near = [
            axial_flux([x_ref[base + step * h, c, at, :] for c in range(COMPONENTS)]) for h in range(REACH)
        ]
        for (first, count), out in zip(SENDS[1:], outs):
            for n in range(count):
                for c in range(COMPONENTS):
                    out[n, c, at, :] = border_terms(near, forward, first + n, c)


def inner_kernel(x_ref, t_ref, pack_ref):
    stations, _, rows, width = x_ref.shape
    forward = lax.rem(lax.axis_index("ax"), 2) == 1
    base = jnp.where(forward, 0, REACH - 1)
    step = jnp.where(forward, 1, -1)
    halo_terms(x_ref, base, step, forward, [(0, stations)], [t_ref])
    groups = rows // TILE
    lane = lax.broadcasted_iota(jnp.int32, (TILE, LANES), 1)
    span = pack_ref.shape[0] // COMPONENTS
    for c in range(COMPONENTS):
        edge = jnp.zeros((TILE, LANES), jnp.float32)
        for s in range(stations):
            pack_ref[c * span + s * REACH : c * span + (s + 1) * REACH, :] = x_ref[s, c, 0:REACH, :]
            for g in range(groups):
                place = (s * groups + g) * 2 * REACH
                first = x_ref[s, c, g * TILE : (g + 1) * TILE, 0:LANES]
                final = x_ref[s, c, g * TILE : (g + 1) * TILE, width - LANES : width]
                both = pltpu.roll(jnp.where(lane < REACH, first, final), (place + REACH) % LANES, 1)
                edge = jnp.where((lane >= place) & (lane < place + 2 * REACH), both, edge)
        height = TILE * LANES // width
        start = (c + 1) * span - height
        for i in range(width // LANES):
            pack_ref[start : start + height, i * LANES : (i + 1) * LANES] = edge[i * height : (i + 1) * height]


def base_kernel(
    turn, x_ref, inner_ref, own_ref, left_ref, right_ref, across_ref, table_ref, back_ref, modes_ref, limit_ref,
    base_ref, weight_ref, inside_ref, basis_ref, unbasis_ref, radial_ref, axial_ref,
):
    stations, _, rows, width = x_ref.shape
    points = int(round(turn))
    groups = rows // TILE
    lane = lax.broadcasted_iota(jnp.int32, (TILE, LANES), 1)
    span = own_ref.shape[0] // COMPONENTS
    height = TILE * LANES // width

    def edge_of(ref, c):
        start = (c + 1) * span - height
        parts = [
            ref[start : start + height, i * LANES : (i + 1) * LANES] for i in range(width // LANES)
        ]
        return parts[0] if len(parts) == 1 else jnp.concatenate(parts, axis=0)

    per_angle = turn / (2.0 * math.pi)

    slot = lane % (2 * REACH)
    from_left = slot < REACH

    def edge_flux(s):
        _, _, vel, p = primitives(s)
        return flux(s, vel, p, 3)

    own = edge_flux([edge_of(own_ref, c) for c in range(COMPONENTS)])
    other = edge_flux(
        [
            jnp.where(from_left, edge_of(left_ref, c), edge_of(right_ref, c))
            for c in range(COMPONENTS)
        ]
    )
    fixes = []
    for c in range(COMPONENTS):
        change = other[c] - own[c]
        fix = jnp.zeros((TILE, LANES), jnp.float32)
        for k in range(1, REACH + 1):
            ahead = pltpu.roll(change, LANES - k, 1)
            behind = pltpu.roll(change, k, 1)
            fix = fix + STENCIL[k - 1] * jnp.where(
                from_left,
                jnp.where(slot + k >= REACH, ahead, 0.0),
                jnp.where(slot - k < REACH, -behind, 0.0),
            )
        fixes.append(fix)

    for s in range(stations):
        cross = [across_ref[c * span + s * REACH : c * span + (s + 1) * REACH, :] for c in range(COMPONENTS)]
        _, vel, _, p = primitives(cross)
        far = flux(cross, vel, p, 2)
        for c in range(COMPONENTS):
            sign = -1.0 if c in (2, 3) else 1.0
            for i in range(REACH):
                radial_ref[s, c, TILE - 1 - i : TILE - i, :] = (sign * (i + 0.5)) * far[c][i : i + 1, :]
        for g in range(groups):
            at = slice(g * TILE, (g + 1) * TILE)
            state = [x_ref[s, c, at, :] for c in range(COMPONENTS)]
            a, b, vel, p = primitives(state)
            ahead = flux(state, a, p, 1)
            out = flux(state, b, p, 2)
            swirl = flux(state, vel, p, 3)
            radius = (
                lax.broadcasted_iota(jnp.int32, (TILE, width), 0).astype(jnp.float32) + (g * TILE + 0.5)
            )
            for c in range(COMPONENTS):
                axial_ref[s, c, at, :] = TIME_STEP * ahead[c]
                radial_ref[s, c, TILE + g * TILE : TILE + (g + 1) * TILE, :] = radius * out[c]
                if g == groups - 1:
                    edge = out[c][TILE - 1 : TILE, :]
                    for m in range(1, REACH + 1):
                        radial_ref[s, c, TILE + rows + m - 1 : TILE + rows + m, :] = (rows - 0.5 + m) * edge
            place = (s * groups + g) * 2 * REACH
            source = {2: state[3] * vel + p, 3: -(state[2] * vel)}
            for c in range(COMPONENTS):
                turned = None
                for k in range(1, REACH + 1):
                    part = STENCIL[k - 1] * (
                        pltpu.roll(swirl[c], width - k, 1) - pltpu.roll(swirl[c], k, 1)
                    )
                    turned = part if turned is None else turned + part
                fix = pltpu.roll(fixes[c], (LANES - REACH - place) % LANES, 1)
                head = jnp.where(lane < REACH, fix, 0.0)
                tail = jnp.where(lane >= LANES - REACH, fix, 0.0)
                if width == LANES:
                    turned = turned + (head + tail)
                else:
                    middle = [jnp.zeros((TILE, width - 2 * LANES), jnp.float32)] if width > 2 * LANES else []
                    turned = turned + jnp.concatenate([head] + middle + [tail], axis=1)
                total = per_angle * turned
                if c in source:
                    total = total - source[c]
                base_ref[s, c, at, :] = total
    for g in range(groups):
        at = slice(g * TILE, (g + 1) * TILE)
        start = TILE + g * TILE
        radius = lax.broadcasted_iota(jnp.int32, (TILE, width), 0).astype(jnp.float32) + (g * TILE + 0.5)
        scale = TIME_STEP / radius
        for c in range(COMPONENTS):
            near = [axial_ref[h, c, at, :] for h in range(stations)]
            for s in range(stations):
                total = base_ref[s, c, at, :]
                for k in range(1, REACH + 1):
                    total = total + STENCIL[k - 1] * (
                        radial_ref[s, c, start + k : start + k + TILE, :]
                        - radial_ref[s, c, start - k : start - k + TILE, :]
                    )
                total = x_ref[s, c, at, :] + inner_ref[s, c, at, :] - scale * total
                for h in range(stations):
                    if h != s:
                        total = total + (STENCIL[abs(h - s) - 1] * (-1.0 if h > s else 1.0)) * near[h]
                base_ref[s, c, at, :] = total

    sector = lax.axis_index("az")
    basis_ref[0], basis_ref[1] = halves(table_ref[sector])
    unbasis_ref[0], unbasis_ref[1] = halves(back_ref[sector])
    line = lax.broadcasted_iota(jnp.int32, (rows, LANES), 0)
    for s in range(stations):
        inside_ref[s] = (line < limit_ref[s]).astype(jnp.float32)
    columns = 2 * MODE_MOST
    harmonic = lax.broadcasted_iota(jnp.int32, (rows, columns), 1) % MODE_MOST
    row = lax.broadcasted_iota(jnp.int32, (rows, columns), 0)
    kept = jnp.zeros((rows, columns), jnp.int32)
    for j in range(rows):
        kept = jnp.where(row == j, modes_ref[j], kept)
    weight = jnp.where(harmonic == 0, 1.0 / points, 2.0 / points).astype(jnp.float32)
    weight_ref[...] = jnp.where(harmonic < kept, weight, 0.0)


def forward_kernel(n, last, base_ref, basis_ref, *refs):
    section_ref, coeff_ref = refs[-2:]
    first, count = GROUPS[n]
    width = base_ref.shape[-1]
    me = lax.axis_index("ax")
    end = (me == 0) | (me == last)
    inside = [(a, m) for a, m in SENDS if first <= a < first + count]
    for i, (a, m) in enumerate(inside):
        for k in range(m):
            terms = jnp.where(end, refs[2 * i][k], refs[2 * i + 1][k])
            section_ref[a - first + k] = base_ref[place_of(a + k)] + terms
    coeff_ref[...] = close_dot(section_ref[...].reshape(-1, width), basis_ref[0], basis_ref[1])


def smooth(total, section, weight, unbasis, inside):
    _, rows, width = section.shape
    kept = (total.reshape(COMPONENTS, rows, -1) * weight[None]).reshape(COMPONENTS * rows, -1)
    value = close_dot(kept, unbasis[0], unbasis[1]).reshape(section.shape)
    pick = (inside > 0.5)[None]
    return [
        jnp.where(pick, value[:, :, t : t + LANES], section[:, :, t : t + LANES]) for t in range(0, width, LANES)
    ]


def inverse_kernel(n, section_ref, mine_ref, other_ref, weight_ref, unbasis_ref, inside_ref, *refs):
    first, count = GROUPS[n]
    copies = []
    if n == LAST:
        done, (out_ref, target, sem) = refs[:LAST], refs[LAST:]
        for i, ref in enumerate(done):
            a, m = GROUPS[i]
            for k in range(m):
                copies.append(pltpu.make_async_copy(ref.at[k], out_ref.at[place_of(a + k)], sem.at[a + k]))
        for copy in copies:
            copy.start()
    else:
        (target,) = refs
    lines = COMPONENTS * section_ref.shape[2]
    for s in range(count):
        part = slice(s * lines, (s + 1) * lines)
        total = mine_ref[part, :] + other_ref[part, :]
        parts = smooth(total, section_ref[s], weight_ref[...], unbasis_ref[...], inside_ref[place_of(first + s)])
        for i, value in enumerate(parts):
            target[s, :, :, i * LANES : (i + 1) * LANES] = value
    if n == LAST:
        for s in range(count):
            copies.append(
                pltpu.make_async_copy(target.at[s], out_ref.at[place_of(first + s)], sem.at[first + s])
            )
            copies[-1].start()
        for copy in copies:
            copy.wait()


def fourier_tables(sectors, width):
    points = sectors * width
    harmonic = np.arange(2 * MODE_MOST) % MODE_MOST
    angle = (np.arange(points)[:, None] * harmonic[None, :] % points) * (2.0 * np.pi / points)
    table = np.where(np.arange(2 * MODE_MOST)[None, :] < MODE_MOST, np.cos(angle), np.sin(angle))
    return table.astype(np.float32).reshape(sectors, width, 2 * MODE_MOST)


def per_device_inner(conserved, cycle_modes, filtered_cycles):
    line = lax.axis_size("ax")
    sectors = lax.axis_size("az")
    stations, components, rows, width = conserved.shape
    if stations != REACH or components != COMPONENTS or line % 2 or sectors % 2:
        raise ValueError("unsupported shape")
    if (stations * rows // TILE) * 2 * REACH > LANES or width % LANES or rows % TILE:
        raise ValueError("unsupported shape")
    struct = lambda *shape: jax.ShapeDtypeStruct(shape, jnp.float32)
    block = struct(*conserved.shape)
    params = pltpu.CompilerParams(**PARAMS)
    columns = 2 * MODE_MOST

    def turned(value, by):
        return lax.ppermute(value, "az", [(i, (i + by) % sectors) for i in range(sectors)])

    def others(value):
        return turned(value, 1) if sectors == 2 else lax.psum(value, "az") - value

    def call(kernel, outs, ins, out_specs=None, scratch=(), scalars=0):
        many = isinstance(outs, tuple)
        return pl.pallas_call(
            kernel, out_shape=outs, in_specs=[VMEM] * (len(ins) - scalars) + [SMEM] * scalars,
            out_specs=out_specs or ((VMEM,) * len(outs) if many else VMEM),
            scratch_shapes=scratch, compiler_params=params,
        )(*ins)

    shapes = [struct(count, components, rows, width) for _, count in GROUPS]
    lines = components * rows
    table = fourier_tables(sectors, width)
    forth, back = jnp.asarray(table), jnp.asarray(np.ascontiguousarray(table.transpose(0, 2, 1)))

    pairs = [(i, i + 1) for i in range(1, line - 1, 2)]
    pairs += [(j, i) for i, j in pairs]
    route = [(i * sectors + a, j * sectors + a) for i, j in pairs for a in range(sectors)]
    route += [(i * sectors + a, i * sectors + (a + 1) % sectors) for i in (0, line - 1) for a in range(sectors)]
    sent = [struct(m, components, rows, width) for _, m in SENDS]
    terms = [
        pl.pallas_call(
            functools.partial(first_kernel, line - 1), out_shape=sent[0],
            in_specs=[pl.BlockSpec(memory_space=pltpu.HBM)], out_specs=VMEM,
            scratch_shapes=[pltpu.VMEM(conserved.shape[1:], jnp.float32), pltpu.SemaphoreType.DMA],
            compiler_params=params, name="first",
        )(pltpu.with_memory_space_constraint(conserved, pltpu.HBM))
    ]
    terms += call(functools.partial(outer_kernel, line - 1), tuple(sent[1:]), [conserved])
    inner, pack = call(
        inner_kernel, (block, struct(components * (stations * REACH + TILE * LANES // width), width)), [conserved]
    )
    across = turned(pack, sectors // 2)
    left, right = (across, across) if sectors == 2 else (turned(pack, 1), turned(pack, -1))
    arrived = []
    for value in terms:
        arrived.append(lax.ppermute(value, ("ax", "az"), route))
    inner = lax.ppermute(inner, "ax", [(i, i ^ 1) for i in range(line)])
    base, weight, inside, basis, unbasis = call(
        functools.partial(base_kernel, float(width * sectors)),
        (
            block, struct(rows, columns), struct(stations, rows, LANES),
            jax.ShapeDtypeStruct((2, width, columns), jnp.bfloat16),
            jax.ShapeDtypeStruct((2, columns, width), jnp.bfloat16),
        ),
        [conserved, inner, pack, left, right, across, forth, back, cycle_modes, filtered_cycles],
        scalars=2,
        scratch=[
            pltpu.VMEM((stations, COMPONENTS, rows + 2 * TILE, width), jnp.float32),
            pltpu.VMEM(conserved.shape, jnp.float32),
        ],
    )
    done = []
    for n, (first, count) in enumerate(GROUPS):
        both = []
        for (a, m), own, got in zip(SENDS, terms, arrived):
            if first <= a < first + count:
                both += [own, got]
        section, mine = call(
            functools.partial(forward_kernel, n, line - 1), (shapes[n], struct(count * lines, columns)),
            [base, basis, *both],
        )
        other = others(mine)
        operands = [section, mine, other, weight, unbasis, inside]
        if n < LAST:
            done.append(call(functools.partial(inverse_kernel, n), shapes[n], operands))
    return call(
        functools.partial(inverse_kernel, LAST), block, operands + done, out_specs=ANY,
        scratch=[pltpu.VMEM(shapes[LAST].shape, jnp.float32), pltpu.SemaphoreType.DMA((stations,))],
    )


def solution(mesh):
    placed = (P("ax", None, None, "az"), P(), P("ax"))
    return jax.shard_map(
        per_device_inner, mesh=mesh, in_specs=placed, out_specs=P("ax", None, None, "az"), check_vma=False
    )
```

```python
import functools
import math

import jax
import jax.numpy as jnp
import numpy as np
from jax import lax
from jax.experimental import pallas as pl
from jax.experimental.pallas import tpu as pltpu
from jax.sharding import PartitionSpec as P


MODE_MOST = 64
STENCIL = (0.8, -0.2, 4.0 / 105.0, -1.0 / 280.0)
REACH = len(STENCIL)
GAS_FACTOR = 0.4
TIME_STEP = 0.1
COMPONENTS = 5
TILE = 8
LANES = 128
SENDS = ((0, 1), (1, 1), (2, 1), (3, 1))
GROUPS = ((0, 2), (2, 1), (3, 1))
PIECES = ((0, 2), (2, 4), (4, 5))

VMEM = pl.BlockSpec(memory_space=pltpu.VMEM)
SMEM = pl.BlockSpec(memory_space=pltpu.SMEM)
ANY = pl.BlockSpec(memory_space=pl.ANY)
PARAMS = dict(vmem_limit_bytes=8 << 20)


def halves(value):
    high = value.astype(jnp.bfloat16)
    return high, (value - high.astype(jnp.float32)).astype(jnp.bfloat16)


def close_dot(a, high, low):
    top, rest = halves(a)
    left = jnp.concatenate([top, top, rest], axis=1)
    right = jnp.concatenate([high, low, high], axis=0)
    return lax.dot_general(left, right, (((1,), (0,)), ((), ())), preferred_element_type=jnp.float32)


def primitives(s):
    inverse = 1.0 / s[0]
    a, b, c = s[1] * inverse, s[2] * inverse, s[3] * inverse
    p = GAS_FACTOR * (s[4] - 0.5 * (s[1] * a + s[2] * b + s[3] * c))
    return a, b, c, p


def flux(s, vel, p, along):
    out = [s[along]] + [s[i] * vel for i in (1, 2, 3)] + [vel * (s[4] + p)]
    out[along] = out[along] + p
    return out


def axial_flux(s):
    inverse = 1.0 / s[0]
    a = s[1] * inverse
    p = GAS_FACTOR * (s[4] - 0.5 * ((s[1] * s[1] + s[2] * s[2] + s[3] * s[3]) * inverse))
    return flux(s, a, p, 1)


def halo_terms(x_ref, base, step, forward, chunks, outs):
    rows = x_ref.shape[2]
    scale = jnp.where(forward, -TIME_STEP, TIME_STEP)
    after = [[STENCIL[REACH + h - i - 1] if h <= i else 0.0 for h in range(REACH)] for i in range(REACH)]
    before = [[STENCIL[i + h] if i + h < REACH else 0.0 for h in range(REACH)] for i in range(REACH)]
    for r in range(0, rows, TILE):
        at = slice(r, r + TILE)
        near = []
        for h in range(REACH):
            near.append(axial_flux([x_ref[base + step * h, c, at, :] for c in range(COMPONENTS)]))
        for (first, count), out in zip(chunks, outs):
            for n in range(count):
                i = first + n
                weights = [scale * jnp.where(forward, after[i][h], before[i][h]) for h in range(REACH)]
                for c in range(COMPONENTS):
                    out[n, c, at, :] = sum(w * near[h][c] for h, w in enumerate(weights))


def toward(me, last):
    even = lax.rem(me, 2) == 0
    end = (me == 0) | (me == last)
    base = jnp.where(even, 0, REACH - 1)
    step = jnp.where(end, 0, jnp.where(even, 1, -1))
    return base, step, even != end


def border_terms(near, forward, n, c):
    scale = jnp.where(forward, -TIME_STEP, TIME_STEP)
    return scale * sum(STENCIL[REACH + h - n - 1] * near[h][c] for h in range(n + 1))


def place_of(n):
    return jnp.where(lax.rem(lax.axis_index("ax"), 2) == 0, REACH - 1 - n, n)


def first_kernel(last, x_ref, out_ref, buffer, sem):
    base, _, forward = toward(lax.axis_index("ax"), last)
    copy = pltpu.make_async_copy(x_ref.at[base], buffer, sem)
    copy.start()
    copy.wait()
    for r in range(0, buffer.shape[1], TILE):
        at = slice(r, r + TILE)
        near = [axial_flux([buffer[c, at, :] for c in range(COMPONENTS)])]
        for c in range(COMPONENTS):
            out_ref[0, c, at, :] = border_terms(near, forward, 0, c)


def outer_kernel(last, x_ref, *outs):
    base, step, forward = toward(lax.axis_index("ax"), last)
    for r in range(0, x_ref.shape[2], TILE):
        at = slice(r, r + TILE)
        near = [
            axial_flux([x_ref[base + step * h, c, at, :] for c in range(COMPONENTS)]) for h in range(REACH)
        ]
        for (first, count), out in zip(SENDS[1:], outs):
            for n in range(count):
                for c in range(COMPONENTS):
                    out[n, c, at, :] = border_terms(near, forward, first + n, c)


def inner_kernel(x_ref, t_ref, pack_ref):
    stations, _, rows, width = x_ref.shape
    forward = lax.rem(lax.axis_index("ax"), 2) == 1
    base = jnp.where(forward, 0, REACH - 1)
    step = jnp.where(forward, 1, -1)
    halo_terms(x_ref, base, step, forward, [(0, stations)], [t_ref])
    groups = rows // TILE
    lane = lax.broadcasted_iota(jnp.int32, (TILE, LANES), 1)
    span = pack_ref.shape[0] // COMPONENTS
    for c in range(COMPONENTS):
        edge = jnp.zeros((TILE, LANES), jnp.float32)
        for s in range(stations):
            pack_ref[c * span + s * REACH : c * span + (s + 1) * REACH, :] = x_ref[s, c, 0:REACH, :]
            for g in range(groups):
                place = (s * groups + g) * 2 * REACH
                first = x_ref[s, c, g * TILE : (g + 1) * TILE, 0:LANES]
                final = x_ref[s, c, g * TILE : (g + 1) * TILE, width - LANES : width]
                both = pltpu.roll(jnp.where(lane < REACH, first, final), (place + REACH) % LANES, 1)
                edge = jnp.where((lane >= place) & (lane < place + 2 * REACH), both, edge)
        height = TILE * LANES // width
        start = (c + 1) * span - height
        for i in range(width // LANES):
            pack_ref[start : start + height, i * LANES : (i + 1) * LANES] = edge[i * height : (i + 1) * height]


def base_kernel(
    turn, x_ref, inner_ref, own_ref, left_ref, right_ref, across_ref, table_ref, back_ref, modes_ref, limit_ref,
    base_ref, weight_ref, inside_ref, basis_ref, unbasis_ref, radial_ref, axial_ref,
):
    stations, _, rows, width = x_ref.shape
    points = int(round(turn))
    groups = rows // TILE
    lane = lax.broadcasted_iota(jnp.int32, (TILE, LANES), 1)
    span = own_ref.shape[0] // COMPONENTS
    height = TILE * LANES // width

    def edge_of(ref, c):
        start = (c + 1) * span - height
        parts = [
            ref[start : start + height, i * LANES : (i + 1) * LANES] for i in range(width // LANES)
        ]
        return parts[0] if len(parts) == 1 else jnp.concatenate(parts, axis=0)

    per_angle = turn / (2.0 * math.pi)

    slot = lane % (2 * REACH)
    from_left = slot < REACH

    def edge_flux(s):
        _, _, vel, p = primitives(s)
        return flux(s, vel, p, 3)

    own = edge_flux([edge_of(own_ref, c) for c in range(COMPONENTS)])
    other = edge_flux(
        [
            jnp.where(from_left, edge_of(left_ref, c), edge_of(right_ref, c))
            for c in range(COMPONENTS)
        ]
    )
    fixes = []
    for c in range(COMPONENTS):
        change = other[c] - own[c]
        fix = jnp.zeros((TILE, LANES), jnp.float32)
        for k in range(1, REACH + 1):
            ahead = pltpu.roll(change, LANES - k, 1)
            behind = pltpu.roll(change, k, 1)
            fix = fix + STENCIL[k - 1] * jnp.where(
                from_left,
                jnp.where(slot + k >= REACH, ahead, 0.0),
                jnp.where(slot - k < REACH, -behind, 0.0),
            )
        fixes.append(fix)

    for s in range(stations):
        cross = [across_ref[c * span + s * REACH : c * span + (s + 1) * REACH, :] for c in range(COMPONENTS)]
        _, vel, _, p = primitives(cross)
        far = flux(cross, vel, p, 2)
        for c in range(COMPONENTS):
            sign = -1.0 if c in (2, 3) else 1.0
            for i in range(REACH):
                radial_ref[s, c, TILE - 1 - i : TILE - i, :] = (sign * (i + 0.5)) * far[c][i : i + 1, :]
        for g in range(groups):
            at = slice(g * TILE, (g + 1) * TILE)
            state = [x_ref[s, c, at, :] for c in range(COMPONENTS)]
            a, b, vel, p = primitives(state)
            ahead = flux(state, a, p, 1)
            out = flux(state, b, p, 2)
            swirl = flux(state, vel, p, 3)
            radius = (
                lax.broadcasted_iota(jnp.int32, (TILE, width), 0).astype(jnp.float32) + (g * TILE + 0.5)
            )
            for c in range(COMPONENTS):
                axial_ref[s, c, at, :] = TIME_STEP * ahead[c]
                radial_ref[s, c, TILE + g * TILE : TILE + (g + 1) * TILE, :] = radius * out[c]
                if g == groups - 1:
                    edge = out[c][TILE - 1 : TILE, :]
                    for m in range(1, REACH + 1):
                        radial_ref[s, c, TILE + rows + m - 1 : TILE + rows + m, :] = (rows - 0.5 + m) * edge
            place = (s * groups + g) * 2 * REACH
            source = {2: state[3] * vel + p, 3: -(state[2] * vel)}
            for c in range(COMPONENTS):
                turned = None
                for k in range(1, REACH + 1):
                    part = STENCIL[k - 1] * (
                        pltpu.roll(swirl[c], width - k, 1) - pltpu.roll(swirl[c], k, 1)
                    )
                    turned = part if turned is None else turned + part
                fix = pltpu.roll(fixes[c], (LANES - REACH - place) % LANES, 1)
                head = jnp.where(lane < REACH, fix, 0.0)
                tail = jnp.where(lane >= LANES - REACH, fix, 0.0)
                if width == LANES:
                    turned = turned + (head + tail)
                else:
                    middle = [jnp.zeros((TILE, width - 2 * LANES), jnp.float32)] if width > 2 * LANES else []
                    turned = turned + jnp.concatenate([head] + middle + [tail], axis=1)
                total = per_angle * turned
                if c in source:
                    total = total - source[c]
                base_ref[s, c, at, :] = total
    for g in range(groups):
        at = slice(g * TILE, (g + 1) * TILE)
        start = TILE + g * TILE
        radius = lax.broadcasted_iota(jnp.int32, (TILE, width), 0).astype(jnp.float32) + (g * TILE + 0.5)
        scale = TIME_STEP / radius
        for c in range(COMPONENTS):
            near = [axial_ref[h, c, at, :] for h in range(stations)]
            for s in range(stations):
                total = base_ref[s, c, at, :]
                for k in range(1, REACH + 1):
                    total = total + STENCIL[k - 1] * (
                        radial_ref[s, c, start + k : start + k + TILE, :]
                        - radial_ref[s, c, start - k : start - k + TILE, :]
                    )
                total = x_ref[s, c, at, :] + inner_ref[s, c, at, :] - scale * total
                for h in range(stations):
                    if h != s:
                        total = total + (STENCIL[abs(h - s) - 1] * (-1.0 if h > s else 1.0)) * near[h]
                base_ref[s, c, at, :] = total

    sector = lax.axis_index("az")
    basis_ref[0], basis_ref[1] = halves(table_ref[sector])
    unbasis_ref[0], unbasis_ref[1] = halves(back_ref[sector])
    line = lax.broadcasted_iota(jnp.int32, (rows, LANES), 0)
    for s in range(stations):
        inside_ref[s] = (line < limit_ref[s]).astype(jnp.float32)
    columns = 2 * MODE_MOST
    harmonic = lax.broadcasted_iota(jnp.int32, (rows, columns), 1) % MODE_MOST
    row = lax.broadcasted_iota(jnp.int32, (rows, columns), 0)
    kept = jnp.zeros((rows, columns), jnp.int32)
    for j in range(rows):
        kept = jnp.where(row == j, modes_ref[j], kept)
    weight = jnp.where(harmonic == 0, 1.0 / points, 2.0 / points).astype(jnp.float32)
    weight_ref[...] = jnp.where(harmonic < kept, weight, 0.0)


def forward_kernel(n, last, base_ref, basis_ref, *refs):
    section_ref, coeff_ref = refs[-2:]
    first, count = GROUPS[n]
    width = base_ref.shape[-1]
    me = lax.axis_index("ax")
    end = (me == 0) | (me == last)
    inside = [(a, m) for a, m in SENDS if first <= a < first + count]
    for i, (a, m) in enumerate(inside):
        for k in range(m):
            terms = jnp.where(end, refs[2 * i][k], refs[2 * i + 1][k])
            section_ref[a - first + k] = base_ref[place_of(a + k)] + terms
    coeff_ref[...] = close_dot(section_ref[...].reshape(-1, width), basis_ref[0], basis_ref[1])


def inverse_kernel(n, section_ref, mine_ref, other_ref, weight_ref, unbasis_ref, inside_ref, *refs):
    first, count = GROUPS[n]
    out_ref, target, sem = refs[-3:]
    rows, width = section_ref.shape[2:]
    lines = COMPONENTS * rows
    copies = []
    for s in range(count):
        here = place_of(first + s)
        inside = (inside_ref[here] > 0.5)[None]
        for low, high in PIECES:
            part = slice(s * lines + low * rows, s * lines + high * rows)
            total = (mine_ref[part, :] + other_ref[part, :]).reshape(high - low, rows, -1)
            kept = (total * weight_ref[...][None]).reshape((high - low) * rows, -1)
            value = close_dot(kept, unbasis_ref[0], unbasis_ref[1]).reshape(high - low, rows, width)
            for t in range(0, width, LANES):
                at = slice(t, t + LANES)
                target[s, low:high, :, at] = jnp.where(inside, value[:, :, at], section_ref[s, low:high, :, at])
            copies.append(
                pltpu.make_async_copy(
                    target.at[s, low:high], out_ref.at[here, low:high], sem.at[len(copies)]
                )
            )
            copies[-1].start()
    for copy in copies:
        copy.wait()


def fourier_tables(sectors, width):
    points = sectors * width
    harmonic = np.arange(2 * MODE_MOST) % MODE_MOST
    angle = (np.arange(points)[:, None] * harmonic[None, :] % points) * (2.0 * np.pi / points)
    table = np.where(np.arange(2 * MODE_MOST)[None, :] < MODE_MOST, np.cos(angle), np.sin(angle))
    return table.astype(np.float32).reshape(sectors, width, 2 * MODE_MOST)


def per_device_inner(conserved, cycle_modes, filtered_cycles):
    line = lax.axis_size("ax")
    sectors = lax.axis_size("az")
    stations, components, rows, width = conserved.shape
    if stations != REACH or components != COMPONENTS or line % 2 or sectors % 2:
        raise ValueError("unsupported shape")
    if (stations * rows // TILE) * 2 * REACH > LANES or width % LANES or rows % TILE:
        raise ValueError("unsupported shape")
    struct = lambda *shape: jax.ShapeDtypeStruct(shape, jnp.float32)
    block = struct(*conserved.shape)
    params = pltpu.CompilerParams(**PARAMS)
    columns = 2 * MODE_MOST

    def turned(value, by):
        return lax.ppermute(value, "az", [(i, (i + by) % sectors) for i in range(sectors)])

    def others(value):
        return turned(value, 1) if sectors == 2 else lax.psum(value, "az") - value

    def call(kernel, outs, ins, out_specs=None, scratch=(), scalars=0):
        many = isinstance(outs, tuple)
        return pl.pallas_call(
            kernel, out_shape=outs, in_specs=[VMEM] * (len(ins) - scalars) + [SMEM] * scalars,
            out_specs=out_specs or ((VMEM,) * len(outs) if many else VMEM),
            scratch_shapes=scratch, compiler_params=params,
        )(*ins)

    shapes = [struct(count, components, rows, width) for _, count in GROUPS]
    lines = components * rows
    table = fourier_tables(sectors, width)
    forth, back = jnp.asarray(table), jnp.asarray(np.ascontiguousarray(table.transpose(0, 2, 1)))

    pairs = [(i, i + 1) for i in range(1, line - 1, 2)]
    pairs += [(j, i) for i, j in pairs]
    route = [(i * sectors + a, j * sectors + a) for i, j in pairs for a in range(sectors)]
    route += [(i * sectors + a, i * sectors + (a + 1) % sectors) for i in (0, line - 1) for a in range(sectors)]
    sent = [struct(m, components, rows, width) for _, m in SENDS]
    terms = [
        pl.pallas_call(
            functools.partial(first_kernel, line - 1), out_shape=sent[0],
            in_specs=[pl.BlockSpec(memory_space=pltpu.HBM)], out_specs=VMEM,
            scratch_shapes=[pltpu.VMEM(conserved.shape[1:], jnp.float32), pltpu.SemaphoreType.DMA],
            compiler_params=params, name="first",
        )(pltpu.with_memory_space_constraint(conserved, pltpu.HBM))
    ]
    terms += call(functools.partial(outer_kernel, line - 1), tuple(sent[1:]), [conserved])
    inner, pack = call(
        inner_kernel, (block, struct(components * (stations * REACH + TILE * LANES // width), width)), [conserved]
    )
    across = turned(pack, sectors // 2)
    left, right = (across, across) if sectors == 2 else (turned(pack, 1), turned(pack, -1))
    arrived = []
    for value in terms:
        arrived.append(lax.ppermute(value, ("ax", "az"), route))
    inner = lax.ppermute(inner, "ax", [(i, i ^ 1) for i in range(line)])
    base, weight, inside, basis, unbasis = call(
        functools.partial(base_kernel, float(width * sectors)),
        (
            block, struct(rows, columns), struct(stations, rows, LANES),
            jax.ShapeDtypeStruct((2, width, columns), jnp.bfloat16),
            jax.ShapeDtypeStruct((2, columns, width), jnp.bfloat16),
        ),
        [conserved, inner, pack, left, right, across, forth, back, cycle_modes, filtered_cycles],
        scalars=2,
        scratch=[
            pltpu.VMEM((stations, COMPONENTS, rows + 2 * TILE, width), jnp.float32),
            pltpu.VMEM(conserved.shape, jnp.float32),
        ],
    )
    done = []
    for n, (first, count) in enumerate(GROUPS):
        both = []
        for (a, m), own, got in zip(SENDS, terms, arrived):
            if first <= a < first + count:
                both += [own, got]
        section, mine = call(
            functools.partial(forward_kernel, n, line - 1), (shapes[n], struct(count * lines, columns)),
            [base, basis, *both],
        )
        other = others(mine)
        operands = [section, mine, other, weight, unbasis, inside]
        out = pl.pallas_call(
            functools.partial(inverse_kernel, n), out_shape=block,
            in_specs=[VMEM] * len(operands) + [ANY] * len(done), out_specs=ANY,
            scratch_shapes=[pltpu.VMEM(shapes[n].shape, jnp.float32), pltpu.SemaphoreType.DMA((count * len(PIECES),))],
            input_output_aliases={len(operands): 0} if done else {},
            compiler_params=params,
        )(*operands, *done)
        done = [out]
    return done[0]


def solution(mesh):
    placed = (P("ax", None, None, "az"), P(), P("ax"))
    return jax.shard_map(
        per_device_inner, mesh=mesh, in_specs=placed, out_specs=P("ax", None, None, "az"), check_vma=False
    )
```

```python
import functools
import math

import jax
import jax.numpy as jnp
import numpy as np
from jax import lax
from jax.experimental import pallas as pl
from jax.experimental.pallas import tpu as pltpu
from jax.sharding import PartitionSpec as P


MODE_MOST = 64
STENCIL = (0.8, -0.2, 4.0 / 105.0, -1.0 / 280.0)
REACH = len(STENCIL)
GAS_FACTOR = 0.4
TIME_STEP = 0.1
COMPONENTS = 5
TILE = 8
LANES = 128
SENDS = ((0, 1), (1, 1), (2, 1), (3, 1))
GROUPS = ((0, 2), (2, 1), (3, 1))
PIECES = ((0, 2), (2, 4), (4, 5))

VMEM = pl.BlockSpec(memory_space=pltpu.VMEM)
SMEM = pl.BlockSpec(memory_space=pltpu.SMEM)
ANY = pl.BlockSpec(memory_space=pl.ANY)
PARAMS = dict(vmem_limit_bytes=8 << 20)


def halves(value):
    high = value.astype(jnp.bfloat16)
    return high, (value - high.astype(jnp.float32)).astype(jnp.bfloat16)


def close_dot(a, high, low):
    top, rest = halves(a)
    left = jnp.concatenate([top, top, rest], axis=1)
    right = jnp.concatenate([high, low, high], axis=0)
    return lax.dot_general(left, right, (((1,), (0,)), ((), ())), preferred_element_type=jnp.float32)


def primitives(s):
    inverse = 1.0 / s[0]
    a, b, c = s[1] * inverse, s[2] * inverse, s[3] * inverse
    p = GAS_FACTOR * (s[4] - 0.5 * (s[1] * a + s[2] * b + s[3] * c))
    return a, b, c, p


def flux(s, vel, p, along):
    out = [s[along]] + [s[i] * vel for i in (1, 2, 3)] + [vel * (s[4] + p)]
    out[along] = out[along] + p
    return out


def axial_flux(s):
    inverse = 1.0 / s[0]
    a = s[1] * inverse
    p = GAS_FACTOR * (s[4] - 0.5 * ((s[1] * s[1] + s[2] * s[2] + s[3] * s[3]) * inverse))
    return flux(s, a, p, 1)


def halo_terms(x_ref, base, step, forward, chunks, outs):
    rows = x_ref.shape[2]
    scale = jnp.where(forward, -TIME_STEP, TIME_STEP)
    after = [[STENCIL[REACH + h - i - 1] if h <= i else 0.0 for h in range(REACH)] for i in range(REACH)]
    before = [[STENCIL[i + h] if i + h < REACH else 0.0 for h in range(REACH)] for i in range(REACH)]
    for r in range(0, rows, TILE):
        at = slice(r, r + TILE)
        near = []
        for h in range(REACH):
            near.append(axial_flux([x_ref[base + step * h, c, at, :] for c in range(COMPONENTS)]))
        for (first, count), out in zip(chunks, outs):
            for n in range(count):
                i = first + n
                weights = [scale * jnp.where(forward, after[i][h], before[i][h]) for h in range(REACH)]
                for c in range(COMPONENTS):
                    out[n, c, at, :] = sum(w * near[h][c] for h, w in enumerate(weights))


def toward(me, last):
    even = lax.rem(me, 2) == 0
    end = (me == 0) | (me == last)
    base = jnp.where(even, 0, REACH - 1)
    step = jnp.where(end, 0, jnp.where(even, 1, -1))
    return base, step, even != end


def border_terms(near, forward, n, c):
    scale = jnp.where(forward, -TIME_STEP, TIME_STEP)
    return scale * sum(STENCIL[REACH + h - n - 1] * near[h][c] for h in range(n + 1))


def place_of(n):
    return jnp.where(lax.rem(lax.axis_index("ax"), 2) == 0, REACH - 1 - n, n)


def first_kernel(last, x_ref, out_ref, buffer, sem):
    base, _, forward = toward(lax.axis_index("ax"), last)
    half = buffer.shape[1] // 2
    copies = [
        pltpu.make_async_copy(x_ref.at[base, :, pl.ds(i * half, half)], buffer.at[:, pl.ds(i * half, half)], sem.at[i])
        for i in (0, 1)
    ]
    for copy in copies:
        copy.start()
    for r in range(0, buffer.shape[1], TILE):
        if r % half == 0:
            copies[r // half].wait()
        at = slice(r, r + TILE)
        near = [axial_flux([buffer[c, at, :] for c in range(COMPONENTS)])]
        for c in range(COMPONENTS):
            out_ref[0, c, at, :] = border_terms(near, forward, 0, c)


def outer_kernel(last, x_ref, *outs):
    base, step, forward = toward(lax.axis_index("ax"), last)
    for r in range(0, x_ref.shape[2], TILE):
        at = slice(r, r + TILE)
        near = [
            axial_flux([x_ref[base + step * h, c, at, :] for c in range(COMPONENTS)]) for h in range(REACH)
        ]
        for (first, count), out in zip(SENDS[1:], outs):
            for n in range(count):
                for c in range(COMPONENTS):
                    out[n, c, at, :] = border_terms(near, forward, first + n, c)


def inner_kernel(x_ref, t_ref, pack_ref):
    stations, _, rows, width = x_ref.shape
    forward = lax.rem(lax.axis_index("ax"), 2) == 1
    base = jnp.where(forward, 0, REACH - 1)
    step = jnp.where(forward, 1, -1)
    halo_terms(x_ref, base, step, forward, [(0, stations)], [t_ref])
    groups = rows // TILE
    lane = lax.broadcasted_iota(jnp.int32, (TILE, LANES), 1)
    span = pack_ref.shape[0] // COMPONENTS
    for c in range(COMPONENTS):
        edge = jnp.zeros((TILE, LANES), jnp.float32)
        for s in range(stations):
            pack_ref[c * span + s * REACH : c * span + (s + 1) * REACH, :] = x_ref[s, c, 0:REACH, :]
            for g in range(groups):
                place = (s * groups + g) * 2 * REACH
                first = x_ref[s, c, g * TILE : (g + 1) * TILE, 0:LANES]
                final = x_ref[s, c, g * TILE : (g + 1) * TILE, width - LANES : width]
                both = pltpu.roll(jnp.where(lane < REACH, first, final), (place + REACH) % LANES, 1)
                edge = jnp.where((lane >= place) & (lane < place + 2 * REACH), both, edge)
        height = TILE * LANES // width
        start = (c + 1) * span - height
        for i in range(width // LANES):
            pack_ref[start : start + height, i * LANES : (i + 1) * LANES] = edge[i * height : (i + 1) * height]


def base_kernel(
    turn, x_ref, inner_ref, own_ref, left_ref, right_ref, across_ref, table_ref, back_ref, modes_ref, limit_ref,
    base_ref, weight_ref, inside_ref, basis_ref, unbasis_ref, radial_ref, axial_ref,
):
    stations, _, rows, width = x_ref.shape
    points = int(round(turn))
    groups = rows // TILE
    lane = lax.broadcasted_iota(jnp.int32, (TILE, LANES), 1)
    span = own_ref.shape[0] // COMPONENTS
    height = TILE * LANES // width

    def edge_of(ref, c):
        start = (c + 1) * span - height
        parts = [
            ref[start : start + height, i * LANES : (i + 1) * LANES] for i in range(width // LANES)
        ]
        return parts[0] if len(parts) == 1 else jnp.concatenate(parts, axis=0)

    per_angle = turn / (2.0 * math.pi)

    slot = lane % (2 * REACH)
    from_left = slot < REACH

    def edge_flux(s):
        _, _, vel, p = primitives(s)
        return flux(s, vel, p, 3)

    own = edge_flux([edge_of(own_ref, c) for c in range(COMPONENTS)])
    other = edge_flux(
        [
            jnp.where(from_left, edge_of(left_ref, c), edge_of(right_ref, c))
            for c in range(COMPONENTS)
        ]
    )
    fixes = []
    for c in range(COMPONENTS):
        change = other[c] - own[c]
        fix = jnp.zeros((TILE, LANES), jnp.float32)
        for k in range(1, REACH + 1):
            ahead = pltpu.roll(change, LANES - k, 1)
            behind = pltpu.roll(change, k, 1)
            fix = fix + STENCIL[k - 1] * jnp.where(
                from_left,
                jnp.where(slot + k >= REACH, ahead, 0.0),
                jnp.where(slot - k < REACH, -behind, 0.0),
            )
        fixes.append(fix)

    for s in range(stations):
        cross = [across_ref[c * span + s * REACH : c * span + (s + 1) * REACH, :] for c in range(COMPONENTS)]
        _, vel, _, p = primitives(cross)
        far = flux(cross, vel, p, 2)
        for c in range(COMPONENTS):
            sign = -1.0 if c in (2, 3) else 1.0
            for i in range(REACH):
                radial_ref[s, c, TILE - 1 - i : TILE - i, :] = (sign * (i + 0.5)) * far[c][i : i + 1, :]
        for g in range(groups):
            at = slice(g * TILE, (g + 1) * TILE)
            state = [x_ref[s, c, at, :] for c in range(COMPONENTS)]
            a, b, vel, p = primitives(state)
            ahead = flux(state, a, p, 1)
            out = flux(state, b, p, 2)
            swirl = flux(state, vel, p, 3)
            radius = (
                lax.broadcasted_iota(jnp.int32, (TILE, width), 0).astype(jnp.float32) + (g * TILE + 0.5)
            )
            for c in range(COMPONENTS):
                axial_ref[s, c, at, :] = TIME_STEP * ahead[c]
                radial_ref[s, c, TILE + g * TILE : TILE + (g + 1) * TILE, :] = radius * out[c]
                if g == groups - 1:
                    edge = out[c][TILE - 1 : TILE, :]
                    for m in range(1, REACH + 1):
                        radial_ref[s, c, TILE + rows + m - 1 : TILE + rows + m, :] = (rows - 0.5 + m) * edge
            place = (s * groups + g) * 2 * REACH
            source = {2: state[3] * vel + p, 3: -(state[2] * vel)}
            for c in range(COMPONENTS):
                turned = None
                for k in range(1, REACH + 1):
                    part = STENCIL[k - 1] * (
                        pltpu.roll(swirl[c], width - k, 1) - pltpu.roll(swirl[c], k, 1)
                    )
                    turned = part if turned is None else turned + part
                fix = pltpu.roll(fixes[c], (LANES - REACH - place) % LANES, 1)
                head = jnp.where(lane < REACH, fix, 0.0)
                tail = jnp.where(lane >= LANES - REACH, fix, 0.0)
                if width == LANES:
                    turned = turned + (head + tail)
                else:
                    middle = [jnp.zeros((TILE, width - 2 * LANES), jnp.float32)] if width > 2 * LANES else []
                    turned = turned + jnp.concatenate([head] + middle + [tail], axis=1)
                total = per_angle * turned
                if c in source:
                    total = total - source[c]
                base_ref[s, c, at, :] = total
    for g in range(groups):
        at = slice(g * TILE, (g + 1) * TILE)
        start = TILE + g * TILE
        radius = lax.broadcasted_iota(jnp.int32, (TILE, width), 0).astype(jnp.float32) + (g * TILE + 0.5)
        scale = TIME_STEP / radius
        for c in range(COMPONENTS):
            near = [axial_ref[h, c, at, :] for h in range(stations)]
            for s in range(stations):
                total = base_ref[s, c, at, :]
                for k in range(1, REACH + 1):
                    total = total + STENCIL[k - 1] * (
                        radial_ref[s, c, start + k : start + k + TILE, :]
                        - radial_ref[s, c, start - k : start - k + TILE, :]
                    )
                total = x_ref[s, c, at, :] + inner_ref[s, c, at, :] - scale * total
                for h in range(stations):
                    if h != s:
                        total = total + (STENCIL[abs(h - s) - 1] * (-1.0 if h > s else 1.0)) * near[h]
                base_ref[s, c, at, :] = total

    sector = lax.axis_index("az")
    basis_ref[0], basis_ref[1] = halves(table_ref[sector])
    unbasis_ref[0], unbasis_ref[1] = halves(back_ref[sector])
    line = lax.broadcasted_iota(jnp.int32, (rows, LANES), 0)
    for s in range(stations):
        inside_ref[s] = (line < limit_ref[s]).astype(jnp.float32)
    columns = 2 * MODE_MOST
    harmonic = lax.broadcasted_iota(jnp.int32, (rows, columns), 1) % MODE_MOST
    row = lax.broadcasted_iota(jnp.int32, (rows, columns), 0)
    kept = jnp.zeros((rows, columns), jnp.int32)
    for j in range(rows):
        kept = jnp.where(row == j, modes_ref[j], kept)
    weight = jnp.where(harmonic == 0, 1.0 / points, 2.0 / points).astype(jnp.float32)
    weight_ref[...] = jnp.where(harmonic < kept, weight, 0.0)


def forward_kernel(n, last, base_ref, basis_ref, *refs):
    section_ref, coeff_ref = refs[-2:]
    first, count = GROUPS[n]
    width = base_ref.shape[-1]
    me = lax.axis_index("ax")
    end = (me == 0) | (me == last)
    inside = [(a, m) for a, m in SENDS if first <= a < first + count]
    for i, (a, m) in enumerate(inside):
        for k in range(m):
            terms = jnp.where(end, refs[2 * i][k], refs[2 * i + 1][k])
            section_ref[a - first + k] = base_ref[place_of(a + k)] + terms
    coeff_ref[...] = close_dot(section_ref[...].reshape(-1, width), basis_ref[0], basis_ref[1])


def inverse_kernel(n, section_ref, mine_ref, other_ref, weight_ref, unbasis_ref, inside_ref, *refs):
    first, count = GROUPS[n]
    out_ref, target, sem = refs[-3:]
    rows, width = section_ref.shape[2:]
    lines = COMPONENTS * rows
    copies = []
    for s in range(count):
        here = place_of(first + s)
        inside = (inside_ref[here] > 0.5)[None]
        for low, high in PIECES:
            part = slice(s * lines + low * rows, s * lines + high * rows)
            total = (mine_ref[part, :] + other_ref[part, :]).reshape(high - low, rows, -1)
            kept = (total * weight_ref[...][None]).reshape((high - low) * rows, -1)
            value = close_dot(kept, unbasis_ref[0], unbasis_ref[1]).reshape(high - low, rows, width)
            for t in range(0, width, LANES):
                at = slice(t, t + LANES)
                target[s, low:high, :, at] = jnp.where(inside, value[:, :, at], section_ref[s, low:high, :, at])
            copies.append(
                pltpu.make_async_copy(
                    target.at[s, low:high], out_ref.at[here, low:high], sem.at[len(copies)]
                )
            )
            copies[-1].start()
    for copy in copies:
        copy.wait()


def fourier_tables(sectors, width):
    points = sectors * width
    harmonic = np.arange(2 * MODE_MOST) % MODE_MOST
    angle = (np.arange(points)[:, None] * harmonic[None, :] % points) * (2.0 * np.pi / points)
    table = np.where(np.arange(2 * MODE_MOST)[None, :] < MODE_MOST, np.cos(angle), np.sin(angle))
    return table.astype(np.float32).reshape(sectors, width, 2 * MODE_MOST)


def per_device_inner(conserved, cycle_modes, filtered_cycles):
    line = lax.axis_size("ax")
    sectors = lax.axis_size("az")
    stations, components, rows, width = conserved.shape
    if stations != REACH or components != COMPONENTS or line % 2 or sectors % 2:
        raise ValueError("unsupported shape")
    if (stations * rows // TILE) * 2 * REACH > LANES or width % LANES or rows % TILE:
        raise ValueError("unsupported shape")
    struct = lambda *shape: jax.ShapeDtypeStruct(shape, jnp.float32)
    block = struct(*conserved.shape)
    params = pltpu.CompilerParams(**PARAMS)
    columns = 2 * MODE_MOST

    def turned(value, by):
        return lax.ppermute(value, "az", [(i, (i + by) % sectors) for i in range(sectors)])

    def others(value):
        return turned(value, 1) if sectors == 2 else lax.psum(value, "az") - value

    def call(kernel, outs, ins, out_specs=None, scratch=(), scalars=0):
        many = isinstance(outs, tuple)
        return pl.pallas_call(
            kernel, out_shape=outs, in_specs=[VMEM] * (len(ins) - scalars) + [SMEM] * scalars,
            out_specs=out_specs or ((VMEM,) * len(outs) if many else VMEM),
            scratch_shapes=scratch, compiler_params=params,
        )(*ins)

    shapes = [struct(count, components, rows, width) for _, count in GROUPS]
    lines = components * rows
    table = fourier_tables(sectors, width)
    forth, back = jnp.asarray(table), jnp.asarray(np.ascontiguousarray(table.transpose(0, 2, 1)))

    pairs = [(i, i + 1) for i in range(1, line - 1, 2)]
    pairs += [(j, i) for i, j in pairs]
    route = [(i * sectors + a, j * sectors + a) for i, j in pairs for a in range(sectors)]
    route += [(i * sectors + a, i * sectors + (a + 1) % sectors) for i in (0, line - 1) for a in range(sectors)]
    sent = [struct(m, components, rows, width) for _, m in SENDS]
    terms = [
        pl.pallas_call(
            functools.partial(first_kernel, line - 1), out_shape=sent[0],
            in_specs=[pl.BlockSpec(memory_space=pltpu.HBM)], out_specs=VMEM,
            scratch_shapes=[pltpu.VMEM(conserved.shape[1:], jnp.float32), pltpu.SemaphoreType.DMA((2,))],
            compiler_params=params, name="first",
        )(pltpu.with_memory_space_constraint(conserved, pltpu.HBM))
    ]
    terms += call(functools.partial(outer_kernel, line - 1), tuple(sent[1:]), [conserved])
    inner, pack = call(
        inner_kernel, (block, struct(components * (stations * REACH + TILE * LANES // width), width)), [conserved]
    )
    across = turned(pack, sectors // 2)
    left, right = (across, across) if sectors == 2 else (turned(pack, 1), turned(pack, -1))
    arrived = []
    for value in terms:
        arrived.append(lax.ppermute(value, ("ax", "az"), route))
    inner = lax.ppermute(inner, "ax", [(i, i ^ 1) for i in range(line)])
    base, weight, inside, basis, unbasis = call(
        functools.partial(base_kernel, float(width * sectors)),
        (
            block, struct(rows, columns), struct(stations, rows, LANES),
            jax.ShapeDtypeStruct((2, width, columns), jnp.bfloat16),
            jax.ShapeDtypeStruct((2, columns, width), jnp.bfloat16),
        ),
        [conserved, inner, pack, left, right, across, forth, back, cycle_modes, filtered_cycles],
        scalars=2,
        scratch=[
            pltpu.VMEM((stations, COMPONENTS, rows + 2 * TILE, width), jnp.float32),
            pltpu.VMEM(conserved.shape, jnp.float32),
        ],
    )
    done = []
    for n, (first, count) in enumerate(GROUPS):
        both = []
        for (a, m), own, got in zip(SENDS, terms, arrived):
            if first <= a < first + count:
                both += [own, got]
        section, mine = call(
            functools.partial(forward_kernel, n, line - 1), (shapes[n], struct(count * lines, columns)),
            [base, basis, *both],
        )
        other = others(mine)
        operands = [section, mine, other, weight, unbasis, inside]
        out = pl.pallas_call(
            functools.partial(inverse_kernel, n), out_shape=block,
            in_specs=[VMEM] * len(operands) + [ANY] * len(done), out_specs=ANY,
            scratch_shapes=[pltpu.VMEM(shapes[n].shape, jnp.float32), pltpu.SemaphoreType.DMA((count * len(PIECES),))],
            input_output_aliases={len(operands): 0} if done else {},
            compiler_params=params,
        )(*operands, *done)
        done = [out]
    return done[0]


def solution(mesh):
    placed = (P("ax", None, None, "az"), P(), P("ax"))
    return jax.shard_map(
        per_device_inner, mesh=mesh, in_specs=placed, out_specs=P("ax", None, None, "az"), check_vma=False
    )
```
